32 devices in a mesh: groups: 2 (over y), seq: 4 (over z), tensor: 2 (over x), sub: 2 (over core).
Axes of the slice: x: 2, y: 2, z: 4, core: 2. Of those that a mesh axis runs over, the one named last changes fastest.
Arguments:
- queries: bfloat16 [8192, 2, 4096], P(('groups', 'seq', 'tensor'), 'sub'), parts along dimension 0, may hold values from -52 to 52
- image_keys: bfloat16 [48, 64, 2, 4096], P(('groups', 'seq'), None, 'sub', 'tensor'), parts along dimension 0, may hold values from -12 to 12
- image_values: bfloat16 [48, 64, 2, 4096], P(('groups', 'seq'), None, 'sub', 'tensor'), parts along dimension 0, may hold values from -6 to 6
- head_gate: float32 [2, 32], P('sub', 'tensor'), may hold values from -1.5 to 1.5
- token_image: int32 [8192], P(('groups', 'seq')), parts along dimension 0, may hold values from 0 to 23, as said below
- span_first: int32 [8192], P(('groups', 'seq')), parts along dimension 0, may hold values from 0 to 23, as said below
- image_slot: int32 [48], P('groups'), parts along dimension 0, may hold values from 0 to 23, as said below
Outputs:
- attended: bfloat16 [8192, 2, 4096], P(('groups', 'seq'), 'sub', 'tensor'), parts along dimension 0
The draws below stay inside these ranges and needn't reach their ends.
There are 2 independent parts, one for each index of `groups`. The reference program is written for one: setup_inputs(seed, part) draws one part's arguments, and reference() takes and returns one part's arrays. A program takes and returns all parts, laid end to end along the dimension named above; an argument that names none is the same for every part. Nothing has to cross between parts.
Inputs may be any that keep to these rules, and one draw needn't show every extreme that they name: Every index of seq holds whole documents, and its first token is the position of an image. token_image[t] is the last image at or before token t, so token_image never falls; the tokens of one index of seq read at most 16 images, and those of some index read exactly 16. Documents begin at images and never cross from one index of seq to the next; span_first[t] <= token_image[t]. A permutation. Image j is held by index image_slot[j] // 6 of seq. The images, in reading order, are dealt to the indices of seq in turn, in an order of the indices drawn for each part; so the tokens of one index of seq read at most 4 image from any one holder, and exactly 4 from some holder.
All inputs are finite; a program needn't handle non-finite values.
Results may differ from the reference program's by a relative error of at most 0.0024.
Values may be sent and summed in bfloat16 or wider, within the bound.
A program may use at most 192 MiB of HBM per device.

```python
import math
import jax
import jax.numpy as jnp
from jax import lax

H = 64
DH = 128
LAT = 64
TOK_DEV = 1024
IMG_DEV = 6
MAXIMG = 16
TOKENS = 4096
IMAGES = 24
N_SEQ = 4
N_SUB = 2


def layout(key):
    base_key = jax.random.fold_in(key, 101)
    key_force, key_slots, key_pos, key_doc, key_order = jax.random.split(base_key, 5)
    key_within = jax.random.fold_in(base_key, 7)
    forced = jax.random.randint(key_force, (), 0, N_SEQ)
    extra_units = IMAGES - MAXIMG - (N_SEQ - 1)
    slot_room = (N_SEQ - 1) * (MAXIMG - 2)
    chosen = jax.random.permutation(key_slots, slot_room)[:extra_units]
    other_shard = chosen // (MAXIMG - 2)
    other_counts = 1 + jnp.sum((other_shard[:, None] == jnp.arange(N_SEQ - 1)[None, :]).astype(jnp.int32), axis=0)
    shard_ids = jnp.arange(N_SEQ, dtype=jnp.int32)
    pick_index = jnp.clip(shard_ids - (shard_ids > forced).astype(jnp.int32), 0, N_SEQ - 2)
    counts = jnp.where(shard_ids == forced, MAXIMG, other_counts[pick_index]).astype(jnp.int32)
    first_ids = (jnp.cumsum(counts) - counts).astype(jnp.int32)
    image_ids = jnp.arange(IMAGES, dtype=jnp.int32)
    img_shard = (jnp.sum((first_ids[None, :] <= image_ids[:, None]).astype(jnp.int32), axis=1) - 1).astype(jnp.int32)
    img_rank = image_ids - first_ids[img_shard]
    pos_keys = jax.random.split(key_pos, N_SEQ)
    drawn_pos = jax.vmap(lambda pos_key: jax.random.permutation(pos_key, TOK_DEV - 1)[:MAXIMG - 1] + 1)(pos_keys)
    usable = jnp.arange(MAXIMG - 1)[None, :] < counts[:, None] - 1
    drawn_pos = jnp.sort(jnp.where(usable, drawn_pos, TOK_DEV), axis=1)
    pos_table = jnp.concatenate([jnp.zeros((N_SEQ, 1), jnp.int32), drawn_pos.astype(jnp.int32)], axis=1)
    position = img_shard * TOK_DEV + pos_table[img_shard, img_rank]
    token_ids = jnp.arange(TOKENS, dtype=jnp.int32)
    token_image = (jnp.sum((position[None, :] <= token_ids[:, None]).astype(jnp.int32), axis=1) - 1).astype(jnp.int32)
    starts = (img_rank == 0) | (jax.random.randint(key_doc, (IMAGES,), 0, 10) < 3)
    doc_first = lax.cummax(jnp.where(starts, image_ids, 0), axis=0).astype(jnp.int32)
    span_first = doc_first[token_image].astype(jnp.int32)
    owner_order = jax.random.permutation(key_order, N_SEQ).astype(jnp.int32)
    within_keys = jax.random.split(key_within, N_SEQ)
    within = jax.vmap(lambda one_key: jax.random.permutation(one_key, IMG_DEV))(within_keys).astype(jnp.int32)
    owner = owner_order[image_ids % N_SEQ]
    image_row = (owner * IMG_DEV + within[owner, image_ids // N_SEQ]).astype(jnp.int32)
    return (token_image, span_first, image_row)


def draw_token_image(key, part):
    return layout(key)[0]


def draw_span_first(key, part):
    return layout(key)[1]


def draw_image_slot(key, part):
    return layout(key)[2]


def draw_queries(key, part):
    own_key = jax.random.fold_in(key, 3)
    key_normal, key_scale = jax.random.split(own_key, 2)
    row_scale = jnp.exp(jax.random.uniform(key_scale, (TOKENS, 1, 1), minval=math.log(0.3), maxval=math.log(3.0)))
    values = jnp.clip(jax.random.normal(key_normal, (TOKENS, H, DH)), -4.0, 4.0) * row_scale
    return values.reshape(TOKENS, N_SUB, H * DH // N_SUB).astype(jnp.bfloat16)


def draw_image_keys(key, part):
    own_key = jax.random.fold_in(key, 5)
    key_normal, key_scale = jax.random.split(own_key, 2)
    row_scale = jnp.exp(jax.random.uniform(key_scale, (IMAGES, LAT, 1, 1), minval=math.log(0.3), maxval=math.log(3.0)))
    values = jnp.clip(jax.random.normal(key_normal, (IMAGES, LAT, H, DH)), -4.0, 4.0) * row_scale
    return values.reshape(IMAGES, LAT, N_SUB, H * DH // N_SUB).astype(jnp.bfloat16)


def level_of(rng, extent, cuts, least, high):
    level, own = 1.0, jax.random.fold_in(rng, 6)
    for axis_at, shards_of in cuts:
        heights = jnp.exp(jax.random.uniform(jax.random.fold_in(own, axis_at), (shards_of,), jnp.float32, least / len(cuts), high / len(cuts)))
        level = level * jnp.repeat(heights, extent[axis_at] // shards_of).reshape([-1 if axis == axis_at else 1 for axis in range(len(extent))])
    return level


def bell_draw(rng, shape, width, bound, cuts=(), kind=jnp.bfloat16):
    entries = jax.random.normal(rng, shape, jnp.float32) * width
    if len(cuts) > 0:
        entries = level_of(rng, shape, cuts, -0.22, 0.18) * entries
    return jnp.clip(entries, min=-bound, max=bound).astype(kind)


def setup_inputs(seed: int = 0, part: int = 0) -> dict:
    arg_keys = jax.random.split(jax.random.key(seed), 8)
    own_keys = jax.random.split(jax.random.fold_in(arg_keys[7], part), 8)
    queries = draw_queries(jax.random.fold_in(jax.random.fold_in(arg_keys[7], part), 71), part)
    image_keys = draw_image_keys(jax.random.fold_in(jax.random.fold_in(arg_keys[7], part), 71), part)
    image_values = bell_draw(own_keys[2], (IMAGES, LAT, N_SUB, H * DH // N_SUB), 1.0, 6.0, ((0, 4), (2, 2), (3, 2)))
    head_gate = jnp.clip(jax.random.uniform(arg_keys[3], (N_SUB, H // N_SUB), jnp.float32, -1.5, 1.5) * level_of(arg_keys[3], (N_SUB, H // N_SUB), ((0, 2), (1, 2)), -0.4, 0.0), -1.5, 1.5)
    token_image = draw_token_image(jax.random.fold_in(jax.random.fold_in(arg_keys[7], part), 71), part)
    span_first = draw_span_first(jax.random.fold_in(jax.random.fold_in(arg_keys[7], part), 71), part)
    image_slot = draw_image_slot(jax.random.fold_in(jax.random.fold_in(arg_keys[7], part), 71), part)
    return dict(queries=queries, image_keys=image_keys, image_values=image_values, head_gate=head_gate, token_image=token_image, span_first=span_first, image_slot=image_slot)


def reference(queries, image_keys, image_values, head_gate, token_image, span_first, image_slot):
    score_scale = 1.0 / math.sqrt(DH)
    query_blocks = queries.reshape(N_SEQ, TOK_DEV, H, DH)
    keys_all = image_keys.reshape(IMAGES, LAT, H, DH)
    values_all = image_values.reshape(IMAGES, LAT, H, DH)
    gate_values = jnp.tanh(head_gate.reshape(H))
    image_blocks = token_image.reshape(N_SEQ, TOK_DEV)
    first_blocks = span_first.reshape(N_SEQ, TOK_DEV)

    def one_shard(inputs):
        q_block, img_block, first_block = inputs
        window_start = jnp.minimum(img_block[0], IMAGES - MAXIMG).astype(jnp.int32)
        window_ids = window_start + jnp.arange(MAXIMG, dtype=jnp.int32)
        window_slots = image_slot[window_ids]
        keys_window = keys_all[window_slots].reshape(MAXIMG * LAT, H, DH).astype(jnp.float32)
        values_window = values_all[window_slots].reshape(MAXIMG * LAT, H, DH).astype(jnp.float32)
        visible = (window_ids[None, :] >= first_block[:, None]) & (window_ids[None, :] <= img_block[:, None])
        key_mask = jnp.repeat(visible, LAT, axis=1)[:, None, :]
        scores = jnp.einsum('thd,khd->thk', q_block.astype(jnp.float32), keys_window) * score_scale
        row_top = lax.optimization_barrier(jnp.max(jnp.where(key_mask, scores, -1e+30), axis=2, keepdims=True))
        raised = jnp.exp(jnp.where(key_mask, scores - row_top, -1e+30))
        row_total = lax.optimization_barrier(jnp.sum(raised, axis=2))
        weights = lax.optimization_barrier(raised.astype(jnp.bfloat16))
        summed = jnp.einsum('thk,khd->thd', weights.astype(jnp.float32), values_window)
        mixed = summed / row_total[..., None] * gate_values[None, :, None]
        return mixed.astype(jnp.bfloat16)
    attended = lax.map(one_shard, (query_blocks, image_blocks, first_blocks))
    return attended.reshape(TOKENS, N_SUB, H * DH // N_SUB)
```

```python
import functools
import math

import jax
import jax.numpy as jnp
from jax import lax
from jax.experimental import pallas as pl
from jax.experimental.pallas import tpu as pltpu
from jax.sharding import PartitionSpec as P

DH = 128
MAXIMG = 16
TILE = 256
LEAD = 3
AHEAD = 1
FEED_AHEAD = 8
PAIRS_AHEAD = 2
FEW = 2
MESH = pl.DeviceIdType.MESH


def fused_kernel(
    plan, held, latents, images,
    slot_ref, tok_ref, gate_ref, last_ref, first_ref, q_ref, k_ref, v_ref, out_ref, *scratch
):
    chunks = len(plan)
    starts = [sum(plan[:c]) * DH for c in range(chunks)]
    widths = [heads * DH for heads in plan]
    own, near, far, farthest, sel, q_all = (
        scratch[part * chunks : (part + 1) * chunks] for part in range(6)
    )
    (win, bias, own_sem, raw_send, raw_recv, rel_send, rel_recv,
     sel_send, sel_recv, q_sem, q_send, q_recv) = scratch[6 * chunks :]
    rows = q_ref.shape[0]
    half = q_ref.shape[1] // 2
    per_holder = MAXIMG // 4
    me = lax.axis_index("seq")
    mine = lax.axis_index("tensor")
    other = 1 - mine
    low = me < 2
    end = jnp.where(low, 0, 3)
    mid = jnp.where(low, 1, 2)
    far_mid = 3 - mid
    far_end = 3 - end
    is_end = me == end
    is_mid = me == mid
    peer = jnp.where(is_end, mid, far_mid)

    barrier = pltpu.get_barrier_semaphore()
    pl.semaphore_signal(barrier, inc=1, device_id={"tensor": other}, device_id_type=MESH)

    @pl.when(is_end)
    def _():
        pl.semaphore_signal(barrier, inc=1, device_id={"seq": mid}, device_id_type=MESH)
        pl.semaphore_wait(barrier, 2)

    @pl.when(is_mid)
    def _():
        pl.semaphore_signal(barrier, inc=1, device_id={"seq": end}, device_id_type=MESH)
        pl.semaphore_signal(barrier, inc=1, device_id={"seq": far_mid}, device_id_type=MESH)
        pl.semaphore_wait(barrier, 3)

    def cols(c):
        return pl.ds(starts[c], widths[c])

    def own_copy(c, kv):
        src = (k_ref, v_ref)[kv]
        return pltpu.make_async_copy(src.at[:, :, cols(c)], own[c].at[kv], own_sem.at[c, kv])

    def raw_copy(c, kv, frm, to):
        src = (k_ref, v_ref)[kv]
        which = 0 if frm is end else 1
        return pltpu.make_async_remote_copy(
            src_ref=src.at[:, :, cols(c)],
            dst_ref=(near, far)[which][c].at[kv],
            send_sem=raw_send.at[c, kv],
            recv_sem=raw_recv.at[which, c, kv],
            device_id={"seq": to},
            device_id_type=MESH,
        )

    def relay_copy(c):
        return pltpu.make_async_remote_copy(
            src_ref=near[c], dst_ref=farthest[c],
            send_sem=rel_send.at[c], recv_sem=rel_recv.at[c],
            device_id={"seq": far_mid}, device_id_type=MESH,
        )

    origins = (mid, far_mid, far_end)

    def sel_copy(c, n):
        return pltpu.make_async_remote_copy(
            src_ref=sel[c].at[:, pl.ds(n * per_holder, per_holder)],
            dst_ref=(near, far, farthest)[n][c].at[:, pl.ds(0, per_holder)],
            send_sem=sel_send.at[c, n],
            recv_sem=sel_recv.at[c, n],
            device_id={"seq": end},
            device_id_type=MESH,
        )

    def q_local(c):
        return pltpu.make_async_copy(
            q_ref.at[:, pl.ds(pl.multiple_of(mine * half + starts[c], DH), widths[c])],
            q_all[c].at[pl.ds(mine * rows, rows)],
            q_sem.at[c],
        )

    def q_remote(c):
        return pltpu.make_async_remote_copy(
            src_ref=q_ref.at[:, pl.ds(pl.multiple_of(other * half + starts[c], DH), widths[c])],
            dst_ref=q_all[c].at[pl.ds(mine * rows, rows)],
            send_sem=q_send.at[c],
            recv_sem=q_recv.at[c],
            device_id={"tensor": other},
            device_id_type=MESH,
        )

    def q_arrival(c):
        return pltpu.make_async_remote_copy(
            src_ref=q_all[c].at[pl.ds(other * rows, rows)],
            dst_ref=q_all[c].at[pl.ds(other * rows, rows)],
            send_sem=q_send.at[c],
            recv_sem=q_recv.at[c],
            device_id={"tensor": other},
            device_id_type=MESH,
        )

    @pl.when(is_end)
    def _():
        for c in range(chunks):
            for kv in range(2):
                raw_copy(c, kv, end, mid).start()

    @pl.when(is_mid)
    def _():
        for c in range(min(2, chunks)):
            for kv in range(2):
                raw_copy(c, kv, mid, far_mid).start()

    for c in range(chunks):
        q_remote(c).start()
    for c in range(chunks):
        for kv in range(2):
            own_copy(c, kv).start()
        q_local(c).start()

    base = jnp.where(
        me == 0, 0, jnp.where(me == 3, images - MAXIMG, jnp.minimum(tok_ref[0], images - MAXIMG))
    )
    neighbour = jnp.where(is_end, mid, end)
    window_rows = []
    for w in range(MAXIMG):
        row = slot_ref[base + w]
        owner = sum(jnp.where(row >= t * held, 1, 0) for t in range(1, 4))
        local = jnp.where(is_end & (owner != me), w // 4, row - owner * held)
        window_rows.append((owner, local))
    end_base = jnp.where(low, 0, images - MAXIMG)
    sel_rows = []
    for origin in origins:
        for k in range(per_holder):
            found = 0
            for t in range(4):
                row = slot_ref[end_base + 4 * k + t]
                inside = (row >= origin * held) & (row < (origin + 1) * held)
                found = found + jnp.where(inside, row - origin * held, 0)
            sel_rows.append(found)

    def send_selected(c, n):
        source = (own, far, farthest)[n][c]
        for at in range(n * per_holder, (n + 1) * per_holder):
            for kv in range(2):
                sel[c][kv, at] = source[kv, sel_rows[at]]
        sel_copy(c, n).start()

    def send_own(c):
        for kv in range(2):
            own_copy(c, kv).wait()
        send_selected(c, 0)

    def pick(c, kv, owner, local):
        image = own[c][kv, local]
        for part, holder in ((near, neighbour), (far, far_mid), (farthest, far_end)):
            image = jnp.where(owner == holder, part[c][kv, local], image)
        return image

    @pl.when(is_mid)
    def _():
        for c in range(LEAD):
            send_own(c)

    tokens = 2 * rows
    ids = base + lax.broadcasted_iota(jnp.int32, (1, MAXIMG * latents), 1) // latents
    for r in range(tokens // DH):
        last = jnp.transpose(jnp.broadcast_to(last_ref[r : r + 1, :], (DH, DH)))
        first = jnp.transpose(jnp.broadcast_to(first_ref[r : r + 1, :], (DH, DH)))
        for at in range(0, MAXIMG * latents, DH):
            part = ids[:, at : at + DH]
            bias[r * DH : (r + 1) * DH, at : at + DH] = jnp.where(
                (part >= first) & (part <= last), 0.0, -1e30
            )
    gates = jnp.tanh(gate_ref[...])
    factor = math.log2(math.e) / math.sqrt(DH)

    for s in range(chunks + 2):
        if s < chunks:
            @pl.when(is_mid)
            def _():
                for kv in range(2):
                    raw_copy(s, kv, end, mid).wait_recv()
                relay_copy(s).start()
                if s + 2 < chunks:
                    for kv in range(2):
                        raw_copy(s + 2, kv, mid, far_mid).start()
        if 0 <= s - 1 < chunks:
            c = s - 1

            @pl.when(is_mid)
            def _():
                for kv in range(2):
                    raw_copy(c, kv, far_mid, mid).wait_recv()
                send_selected(c, 1)
                relay_copy(c).wait_recv()
                send_selected(c, 2)
                if c + LEAD < chunks:
                    send_own(c + LEAD)

        if 0 <= s - 2 < chunks:
            c = s - 2

            @pl.when(is_end)
            def _():
                for kv in range(2):
                    own_copy(c, kv).wait()
                for n in range(3):
                    sel_copy(c, n).wait_recv()

            q_local(c).wait()
            q_arrival(c).wait_recv()
            for w in range(MAXIMG):
                for kv in range(2):
                    win[kv, w * latents : (w + 1) * latents, : widths[c]] = pick(c, kv, *window_rows[w])

            def attend(i, carry):
                at = pl.ds(i * TILE, TILE)
                for h in range(plan[c]):
                    lane = slice(h * DH, (h + 1) * DH)
                    scores = lax.dot_general(
                        q_all[c][at, lane], win[0, :, lane], (((1,), (1,)), ((), ())),
                        preferred_element_type=jnp.float32,
                    ) + bias[at, :]
                    top = jnp.max(scores, axis=1, keepdims=True)
                    raised = jnp.exp2((scores - top) * factor)
                    total = jnp.sum(raised, axis=1, keepdims=True)
                    summed = jnp.dot(
                        raised.astype(jnp.bfloat16), win[1, :, lane],
                        preferred_element_type=jnp.float32,
                    )
                    at_col = starts[c] + h * DH
                    gate = gates[:, at_col // DH : at_col // DH + 1]
                    out_ref[at, at_col : at_col + DH] = (summed * (gate / total)).astype(
                        jnp.bfloat16
                    )
                return carry

            lax.fori_loop(0, tokens // TILE, attend, 0)

    for c in range(chunks):
        q_remote(c).wait_send()

    @pl.when(is_end)
    def _():
        for c in range(chunks):
            for kv in range(2):
                raw_copy(c, kv, end, mid).wait_send()

    @pl.when(is_mid)
    def _():
        for c in range(chunks):
            for kv in range(2):
                raw_copy(c, kv, mid, far_mid).wait_send()
            relay_copy(c).wait_send()
            for n in range(3):
                sel_copy(c, n).wait_send()


def fused(queries, image_keys, image_values, head_gate, token_image, span_first, image_slot):
    rows, _, all_width = queries.shape
    held, latents, _, head_width = image_keys.shape
    images = image_slot.shape[0]
    heads = head_width // DH
    plan = (1, 1) + (2,) * ((heads - 4) // 2) + (1, 1)
    chunks = len(plan)
    widths = [count * DH for count in plan]
    smem = pl.BlockSpec(memory_space=pltpu.SMEM)
    vmem = pl.BlockSpec(memory_space=pltpu.VMEM)
    hbm = pl.BlockSpec(memory_space=pl.ANY)
    dma = pltpu.SemaphoreType.DMA
    out = pl.pallas_call(
        functools.partial(fused_kernel, plan, held, latents, images),
        out_shape=jax.ShapeDtypeStruct((2 * rows, head_width), jnp.bfloat16),
        in_specs=[smem, smem, vmem, vmem, vmem, hbm, hbm, hbm],
        out_specs=vmem,
        scratch_shapes=[pltpu.VMEM((2, held, latents, width), jnp.bfloat16) for width in widths * 4]
        + [pltpu.VMEM((2, 3 * MAXIMG // 4, latents, width), jnp.bfloat16) for width in widths]
        + [pltpu.VMEM((2 * rows, width), jnp.bfloat16) for width in widths]
        + [
            pltpu.VMEM((2, MAXIMG * latents, max(widths)), jnp.bfloat16),
            pltpu.VMEM((2 * rows, MAXIMG * latents), jnp.float32),
            dma((chunks, 2)),
            dma((chunks, 2)),
            dma((2, chunks, 2)),
            dma((chunks,)),
            dma((chunks,)),
            dma((chunks, 3)),
            dma((chunks, 3)),
            dma((chunks,)),
            dma((chunks,)),
            dma((chunks,)),
        ],
        compiler_params=pltpu.CompilerParams(
            collective_id=0, has_side_effects=True, vmem_limit_bytes=44 * 1024 * 1024
        ),
    )(
        image_slot,
        token_image,
        head_gate,
        token_image.reshape(-1, DH),
        span_first.reshape(-1, DH),
        queries.reshape(rows, all_width),
        image_keys.reshape(held, latents, head_width),
        image_values.reshape(held, latents, head_width),
    )
    return out


def offloaded(head):
    return head % 2 == 0


def split_kernel(
    heads, held, latents, images, few,
    slot_ref, gate_ref, last_ref, first_ref, q_ref, k_ref, v_ref, out_ref, flag_ref, *scratch
):
    own, near, far, q_all, q_end = (scratch[part * heads : (part + 1) * heads] for part in range(5))
    (across, toward, results, win, bias, marks, marks_all, flag_out, flag_in,
     mark_send, mark_recv, mark_sem, flag_sem, own_sem, raw_send, raw_recv, x_send, x_recv,
     y_send, y_recv, q_sem, q_send, q_recv, qe_send, qe_recv, o_send, o_recv) = scratch[5 * heads :]
    rows = q_ref.shape[0]
    tokens = 2 * rows
    half = q_ref.shape[1] // 2
    tiles = tokens // TILE
    per_holder = MAXIMG // 4
    big_slots = 2 * per_holder
    me = lax.axis_index("seq")
    mine = lax.axis_index("tensor")
    other = 1 - mine
    group = lax.axis_index("groups")
    low = me < 2
    end = jnp.where(low, 0, 3)
    mid = jnp.where(low, 1, 2)
    far_mid = 3 - mid
    far_end = 3 - end
    is_end = me == end
    is_mid = me == mid
    peers = [lax.rem(me + d, 4) for d in range(1, 4)]

    barrier = pltpu.get_barrier_semaphore()
    pl.semaphore_signal(barrier, inc=1, device_id={"tensor": other}, device_id_type=MESH)
    pl.semaphore_signal(barrier, inc=1, device_id={"groups": 1 - group}, device_id_type=MESH)
    for peer in peers:
        pl.semaphore_signal(barrier, inc=1, device_id={"seq": peer}, device_id_type=MESH)
    marks_all[me, 0:8] = last_ref[...]
    marks_all[me, 8:16] = first_ref[...]
    pl.semaphore_wait(barrier, 5)

    def remote(src, dst, send, recv, **to):
        return pltpu.make_async_remote_copy(
            src_ref=src, dst_ref=dst, send_sem=send, recv_sem=recv, device_id=to, device_id_type=MESH
        )

    def mark_copy(d, row, to):
        return remote(
            marks_all.at[row], marks_all.at[row], mark_send.at[d], mark_recv.at[row], seq=to
        )

    def cols(c):
        return pl.ds(c * DH, DH)

    def own_copy(c, kv):
        return pltpu.make_async_copy((k_ref, v_ref)[kv].at[:, :, cols(c)], own[c].at[kv], own_sem.at[c, kv])

    def raw_copy(c, kv):
        src = (k_ref, v_ref)[kv].at[:, :, cols(c)]
        return remote(src, near[c].at[kv], raw_send.at[c, kv], raw_recv.at[c, kv], seq=mid)

    def cross_copy(c, part):
        at = pl.ds(0, per_holder) if part == 0 else pl.ds(per_holder, per_holder + few)
        return remote(
            across.at[c, :, at], far[c].at[:, at], x_send.at[c, part], x_recv.at[c, part], seq=far_mid
        )

    def toward_copy(c, part):
        first, second = pl.ds(0, per_holder), pl.ds(per_holder, per_holder)
        src, dst = (
            (toward.at[c // 2, :, first], near[c].at[:, first]),
            (far[c].at[:, first], far[c].at[:, first]),
            (toward.at[c // 2, :, second], far[c].at[:, second]),
        )[part]
        return remote(src, dst, y_send.at[c, part], y_recv.at[c, part], seq=end)

    def q_cols(who, c):
        return pl.ds(pl.multiple_of(who * half + c * DH, DH), DH)

    def q_local(c):
        return pltpu.make_async_copy(
            q_ref.at[:, q_cols(mine, c)], q_all[c].at[pl.ds(mine * rows, rows)], q_sem.at[c]
        )

    def q_remote(c):
        return remote(
            q_ref.at[:, q_cols(other, c)], q_all[c].at[pl.ds(mine * rows, rows)],
            q_send.at[c], q_recv.at[c], tensor=other,
        )

    def q_arrival(c):
        landed = q_all[c].at[pl.ds(other * rows, rows)]
        return remote(landed, landed, q_send.at[c], q_recv.at[c], tensor=other)

    def q_lend(c, part):
        who = (mine, other)[part]
        at = pl.ds(who * rows, rows)
        src = q_ref.at[:, q_cols(mine, c)] if part == 0 else q_all[c].at[at]
        return remote(src, q_end[c].at[at], qe_send.at[c // 2, part], qe_recv.at[c // 2, part], seq=mid)

    def result_copy(c, i):
        at = pl.ds(i * TILE, TILE)
        return remote(
            results.at[c // 2, at], results.at[c // 2, at],
            o_send.at[c // 2, i], o_recv.at[c // 2, i], seq=end,
        )

    def send_pair(p):
        for c in (2 * p, 2 * p + 1):
            for kv in range(2):
                raw_copy(c, kv).start()
        q_lend(2 * p, 0).start()
        q_arrival(2 * p).wait_recv()
        q_lend(2 * p, 1).start()

    for d in range(3):
        mark_copy(d, me, peers[d]).start()
    q_remote(0).start()

    @pl.when(is_end)
    def _():
        for c in (0, 1):
            for kv in range(2):
                raw_copy(c, kv).start()
        q_lend(0, 0).start()

    for c in range(1, heads):
        q_remote(c).start()

    @pl.when(is_end)
    def _():
        q_arrival(0).wait_recv()
        q_lend(0, 1).start()
        for p in range(1, PAIRS_AHEAD):
            send_pair(p)
        for c in range(heads):
            if not offloaded(c):
                for kv in range(2):
                    own_copy(c, kv).start()
                q_local(c).start()

    @pl.when(is_mid)
    def _():
        for c in range(heads):
            for kv in range(2):
                own_copy(c, kv).start()
        for c in range(heads):
            q_local(c).start()

    for d in range(3):
        mark_copy(d, peers[d], peers[d]).wait_recv()
    fetch = pltpu.make_async_copy(marks_all, marks, mark_sem)
    fetch.start()
    fetch.wait()

    def owner_of(row):
        return sum(jnp.where(row >= t * held, 1, 0) for t in range(1, 4))

    slots = [slot_ref[j] for j in range(images)]
    owners = [owner_of(row) for row in slots]

    def base_of(i):
        return jnp.minimum(marks[i, 0, 0], images - MAXIMG)

    def side_plan(left):
        one = jnp.where(left, 0, 2)
        spans = []
        for i in (one, one + 1):
            spans.append((jnp.maximum(base_of(i), marks[i, 8, 0]), marks[i, 7, DH - 1]))
        one_big = spans[0][1] - spans[0][0] >= spans[1][1] - spans[1][0]
        big = jnp.where(one_big, one, one + 1)
        lo = jnp.where(one_big, spans[1][0], spans[0][0])
        hi = jnp.where(one_big, spans[1][1], spans[0][1])
        count = 0
        ids = [0] * few
        for j in range(images):
            away = (owners[j] >= 2) == left
            hit = (j >= lo) & (j <= hi) & away
            ids = [jnp.where(hit & (count == n), j, ids[n]) for n in range(few)]
            count = count + jnp.where(hit, 1, 0)
        return big, ids, count

    here_big, here_ids, here_count = side_plan(low)
    there_big, there_ids, there_count = side_plan(jnp.logical_not(low))
    bad = jnp.where((here_count > few) | (there_count > few), 1, 0)
    flag_out[...] = jnp.zeros(flag_out.shape, jnp.int32) + bad
    flag_copy = remote(flag_out, flag_in, flag_sem.at[0], flag_sem.at[1], groups=1 - group)
    flag_copy.start()

    def held_rows(base, origin):
        found_rows = []
        for k in range(per_holder):
            found = 0
            for t in range(4):
                row = slot_ref[base + 4 * k + t]
                inside = (row >= origin * held) & (row < (origin + 1) * held)
                found = found + jnp.where(inside, row - origin * held, 0)
            found_rows.append(jnp.minimum(found, held - 1))
        return found_rows

    def window(i, at_end):
        base = base_of(i)
        is_big = here_big == i
        places = []
        for w in range(MAXIMG):
            row = slot_ref[base + w]
            owner = owner_of(row)
            local = row - owner * held
            away = (owner >= 2) == low
            slot = 0
            for n in range(few - 1, -1, -1):
                slot = jnp.where(here_ids[n] == base + w, n, slot)
            fewer = jnp.where(at_end, per_holder + lax.rem(slot, per_holder), big_slots + slot)
            place = jnp.where(is_big, jnp.where(owner == far_mid, 0, per_holder) + w // 4, fewer)
            beside = jnp.where(at_end, w // 4, local)
            source = jnp.where(away, 2, jnp.where(owner == me, 0, 1))
            places.append((
                source,
                jnp.where(source == 0, local, 0),
                jnp.where(source == 1, beside, 0),
                jnp.where(source == 2, place, 0),
            ))
        return places

    my_window = window(me, is_end)
    end_window = window(end, False)
    there_base = base_of(there_big)
    big_mine = held_rows(there_base, me)
    big_near = held_rows(there_base, end)
    end_mine = held_rows(base_of(end), me)
    few_rows = []
    for n in range(few):
        row = slot_ref[there_ids[n]]
        owner = owner_of(row)
        few_rows.append((owner == me, row - owner * held))
    end_far = [
        jnp.where(here_big == end, per_holder + j, big_slots + j % few) for j in range(per_holder)
    ]

    def lend_own(c):
        for k in range(per_holder):
            for kv in range(2):
                across[c, kv, k] = own[c][kv, big_mine[k]]
        cross_copy(c, 0).start()

    def lend_near(c):
        for k in range(per_holder):
            for kv in range(2):
                across[c, kv, per_holder + k] = near[c][kv, big_near[k]]
        for n in range(few):
            is_own, row = few_rows[n]
            for kv in range(2):
                across[c, kv, big_slots + n] = jnp.where(is_own, own[c][kv, row], near[c][kv, row])
        cross_copy(c, 1).start()

    def feed_own(c):
        for k in range(per_holder):
            for kv in range(2):
                toward[c // 2, kv, k] = own[c][kv, end_mine[k]]
        toward_copy(c, 0).start()

    def feed_far(c):
        for j in range(per_holder):
            for kv in range(2):
                toward[c // 2, kv, per_holder + j] = far[c][kv, end_far[j]]
        toward_copy(c, 2).start()

    own_waited = set()

    def need_own(c):
        if c not in own_waited:
            own_waited.add(c)
            for kv in range(2):
                own_copy(c, kv).wait()

    @pl.when(is_mid)
    def _():
        for c in range(max(AHEAD, FEED_AHEAD)):
            need_own(c)
            if c < AHEAD:
                lend_own(c)
            if c < FEED_AHEAD and not offloaded(c):
                feed_own(c)

    def fill_bias(which, i):
        ids = base_of(i) + lax.broadcasted_iota(jnp.int32, (1, MAXIMG * latents), 1) // latents
        for r in range(tokens // DH):
            last = jnp.transpose(jnp.broadcast_to(marks_all[i, r : r + 1, :], (DH, DH)))
            first = jnp.transpose(jnp.broadcast_to(marks_all[i, 8 + r : 9 + r, :], (DH, DH)))
            for at in range(0, MAXIMG * latents, DH):
                part = ids[:, at : at + DH]
                bias[which, r * DH : (r + 1) * DH, at : at + DH] = jnp.where(
                    (part >= first) & (part <= last), 0.0, -1e30
                )

    fill_bias(0, me)

    @pl.when(is_mid)
    def _():
        fill_bias(1, end)

    gates = jnp.tanh(gate_ref[...])
    factor = math.log2(math.e) / math.sqrt(DH)

    def fill_window(which, c, places):
        for w in range(MAXIMG):
            source, own_row, near_row, far_row = places[w]
            for kv in range(2):
                image = jnp.where(source == 1, near[c][kv, near_row], own[c][kv, own_row])
                win[which, kv, w * latents : (w + 1) * latents] = jnp.where(
                    source == 2, far[c][kv, far_row], image
                )

    def attend(which, q, c, store):
        gate = gates[:, c : c + 1]

        def tile(i, carry):
            at = pl.ds(pl.multiple_of(i * TILE, TILE), TILE)
            scores = lax.dot_general(
                q[at, :], win[which, 0], (((1,), (1,)), ((), ())), preferred_element_type=jnp.float32
            ) + bias[which, at, :]
            top = jnp.max(scores, axis=1, keepdims=True)
            raised = jnp.exp2((scores - top) * factor)
            total = jnp.sum(raised, axis=1, keepdims=True)
            summed = jnp.dot(
                raised.astype(jnp.bfloat16), win[which, 1], preferred_element_type=jnp.float32
            )
            store(i, at, (summed * (gate / total)).astype(jnp.bfloat16))
            return carry

        lax.fori_loop(0, tiles, tile, 0)

    def own_head(c):
        q_local(c).wait()
        q_arrival(c).wait_recv()
        fill_window(0, c, my_window)

        def store(i, at, value):
            out_ref[at, c * DH : (c + 1) * DH] = value

        attend(0, q_all[c], c, store)

    def end_head(c):
        for part in range(2):
            q_lend(c, part).wait_recv()
        fill_window(1, c, end_window)

        def store(i, at, value):
            results[c // 2, at, :] = value
            result_copy(c, i).start()

        attend(1, q_end[c], c, store)

    for s in range(heads + 2):
        c = s - 1
        lent = s - 3

        @pl.when(is_mid)
        def _():
            if s < heads:
                for kv in range(2):
                    raw_copy(s, kv).wait_recv()
                lend_near(s)
                if s + AHEAD < heads:
                    need_own(s + AHEAD)
                    lend_own(s + AHEAD)
                ahead = s + FEED_AHEAD
                if ahead < heads and not offloaded(ahead):
                    need_own(ahead)
                    feed_own(ahead)
                cross_copy(s, 0).wait_recv()
                if not offloaded(s):
                    toward_copy(s, 1).start()
            if 0 <= c < heads:
                cross_copy(c, 1).wait_recv()
                if offloaded(c):
                    own_head(c)
                else:
                    feed_far(c)

        if 0 <= c < heads and not offloaded(c):
            @pl.when(is_end)
            def _():
                if c // 2 + PAIRS_AHEAD < heads // 2:
                    send_pair(c // 2 + PAIRS_AHEAD)
                for kv in range(2):
                    own_copy(c, kv).wait()
                for part in range(3):
                    toward_copy(c, part).wait_recv()

            own_head(c)

        if 0 <= lent < heads and offloaded(lent):
            @pl.when(is_mid)
            def _():
                end_head(lent)

            @pl.when(is_end)
            def _():
                for i in range(tiles):
                    result_copy(lent, i).wait_recv()
                out_ref[:, lent * DH : (lent + 1) * DH] = results[lent // 2]

    flag_copy.wait()
    flag_ref[...] = jnp.maximum(flag_out[...], flag_in[...])
    for d in range(3):
        mark_copy(d, me, peers[d]).wait_send()
    for c in range(heads):
        q_remote(c).wait_send()

    @pl.when(is_end)
    def _():
        for c in range(heads):
            for kv in range(2):
                raw_copy(c, kv).wait_send()
            if offloaded(c):
                for part in range(2):
                    q_lend(c, part).wait_send()

    @pl.when(is_mid)
    def _():
        for c in range(heads):
            for part in range(2):
                cross_copy(c, part).wait_send()
            if offloaded(c):
                for i in range(tiles):
                    result_copy(c, i).wait_send()
            else:
                for part in range(3):
                    toward_copy(c, part).wait_send()


def split(queries, image_keys, image_values, head_gate, token_image, span_first, image_slot):
    rows, _, all_width = queries.shape
    held, latents, _, head_width = image_keys.shape
    images = image_slot.shape[0]
    heads = head_width // DH
    tokens = 2 * rows
    tiles = tokens // TILE
    slots = MAXIMG // 2 + FEW
    smem = pl.BlockSpec(memory_space=pltpu.SMEM)
    vmem = pl.BlockSpec(memory_space=pltpu.VMEM)
    hbm = pl.BlockSpec(memory_space=pl.ANY)
    dma = pltpu.SemaphoreType.DMA
    bf16 = jnp.bfloat16
    return pl.pallas_call(
        functools.partial(split_kernel, heads, held, latents, images, FEW),
        out_shape=(pltpu.VMEM((tokens, head_width), bf16), jax.ShapeDtypeStruct((8, DH), jnp.int32)),
        in_specs=[smem, vmem, vmem, vmem, hbm, hbm, hbm],
        out_specs=(vmem, vmem),
        scratch_shapes=[pltpu.VMEM((2, held, latents, DH), bf16)] * (2 * heads)
        + [pltpu.VMEM((2, slots, latents, DH), bf16)] * heads
        + [pltpu.VMEM((tokens, DH), bf16)] * heads
        + [pltpu.VMEM((tokens if offloaded(c) else 16, DH), bf16) for c in range(heads)]
        + [
            pltpu.VMEM((heads, 2, slots, latents, DH), bf16),
            pltpu.VMEM((heads // 2, 2, MAXIMG // 2, latents, DH), bf16),
            pltpu.VMEM((heads // 2, tokens, DH), bf16),
            pltpu.VMEM((2, 2, MAXIMG * latents, DH), bf16),
            pltpu.VMEM((2, tokens, MAXIMG * latents), jnp.float32),
            pltpu.SMEM((4, 16, DH), jnp.int32),
            pltpu.VMEM((4, 16, DH), jnp.int32),
            pltpu.VMEM((8, DH), jnp.int32),
            pltpu.VMEM((8, DH), jnp.int32),
            dma((3,)),
            dma((4,)),
            dma,
            dma((2,)),
            dma((heads, 2)),
            dma((heads, 2)),
            dma((heads, 2)),
            dma((heads, 2)),
            dma((heads, 2)),
            dma((heads, 3)),
            dma((heads, 3)),
            dma((heads,)),
            dma((heads,)),
            dma((heads,)),
            dma((heads // 2, 2)),
            dma((heads // 2, 2)),
            dma((heads // 2, tiles)),
            dma((heads // 2, tiles)),
        ],
        compiler_params=pltpu.CompilerParams(
            collective_id=1, has_side_effects=True, vmem_limit_bytes=50 * 1024 * 1024
        ),
    )(
        image_slot,
        head_gate,
        token_image.reshape(-1, DH),
        span_first.reshape(-1, DH),
        queries.reshape(rows, all_width),
        image_keys.reshape(held, latents, head_width),
        image_values.reshape(held, latents, head_width),
    )


def attended(*args):
    result, flag = split(*args)
    bad = flag[0, 0]
    kept = jnp.where(bad > 0, jnp.bfloat16(0), result)
    result = lax.while_loop(lambda c: c[0] > 0, lambda c: (0, fused(*args)), (bad, kept))[1]
    return result.reshape(result.shape[0], 1, result.shape[1])


def lookup(lookup_table, at_index):
    count = lookup_table.shape[0]
    hits = jnp.arange(count, dtype=jnp.int32) == at_index[..., None]
    return jnp.sum(jnp.where(hits, lookup_table, 0), axis=-1)


def per_device(queries, image_keys, image_values, head_gate, token_image, span_first, image_slot):
    tensor_count = lax.axis_size("tensor")
    row_count = queries.shape[0]
    half_width = queries.shape[2]
    split_rows = queries.reshape(row_count, tensor_count, half_width // tensor_count)
    head_rows = lax.all_to_all(split_rows, "tensor", split_axis=1, concat_axis=0, tiled=True)
    token_count = head_rows.shape[0]
    head_width = head_rows.shape[2]
    head_count = head_width // DH
    held_count = image_keys.shape[0]
    latents = image_keys.shape[1]
    images = image_slot.shape[0]
    packed = jnp.concatenate([image_keys[:, :, 0, :], image_values[:, :, 0, :]], axis=2)
    packed = packed.reshape(held_count, latents * 2 * head_width)
    window_start = jnp.minimum(token_image[0], images - MAXIMG)
    window_ids = window_start + jnp.arange(MAXIMG, dtype=jnp.int32)
    in_window = window_ids < images
    safe_ids = jnp.minimum(window_ids, images - 1)
    window_slot = lookup(image_slot, safe_ids)
    fragment = lax.all_gather(packed, "seq", axis=0, tiled=True)
    piece_rows = jnp.arange(fragment.shape[0], dtype=jnp.int32)
    select = ((window_slot[:, None] == piece_rows[None, :]) & in_window[:, None]).astype(
        jnp.bfloat16
    )
    window = jnp.dot(select, fragment, preferred_element_type=jnp.float32).astype(jnp.bfloat16)
    window = window.reshape(MAXIMG * latents, 2 * head_width)
    keys_win = window[:, :head_width]
    values_win = window[:, head_width:]
    visible = (window_ids[None, :] >= span_first[:, None]) & (
        window_ids[None, :] <= token_image[:, None]
    )
    key_mask = jnp.repeat(visible, latents, axis=1)
    score_scale = 1.0 / math.sqrt(DH)
    gate_values = jnp.tanh(head_gate.reshape(-1))
    results = []
    for head_index in range(head_count):
        low_col = head_index * DH
        head_query = head_rows[:, 0, low_col : low_col + DH]
        scores = (
            lax.dot_general(
                head_query,
                keys_win[:, low_col : low_col + DH],
                (((1,), (1,)), ((), ())),
                preferred_element_type=jnp.float32,
            )
            * score_scale
        )
        row_top = jnp.max(jnp.where(key_mask, scores, -1e30), axis=1, keepdims=True)
        raised = jnp.exp(jnp.where(key_mask, scores - row_top, -1e30))
        row_total = jnp.sum(raised, axis=1, keepdims=True)
        weights = raised.astype(jnp.bfloat16)
        summed = jnp.dot(
            weights, values_win[:, low_col : low_col + DH], preferred_element_type=jnp.float32
        )
        results.append(summed / row_total * gate_values[head_index])
    attended = jnp.concatenate(results, axis=1).astype(jnp.bfloat16)
    return attended.reshape(token_count, 1, head_width)


def solution(mesh):
    placed = (
        P(("groups", "seq", "tensor"), "sub", None),
        P(("groups", "seq"), None, "sub", "tensor"),
        P(("groups", "seq"), None, "sub", "tensor"),
        P("sub", "tensor"),
        P(("groups", "seq")),
        P(("groups", "seq")),
        P("groups"),
    )
    fits = mesh.shape["seq"] == 4 and mesh.shape["tensor"] == 2
    return jax.shard_map(
        attended if fits else per_device,
        mesh=mesh,
        in_specs=placed,
        out_specs=P(("groups", "seq"), "sub", "tensor"),
        check_vma=False,
    )
```

```python
import functools
import math

import jax
import jax.numpy as jnp
from jax import lax
from jax.experimental import pallas as pl
from jax.experimental.pallas import tpu as pltpu
from jax.sharding import PartitionSpec as P

DH = 128
MAXIMG = 16
TILE = 256
LEAD = 3
AHEAD = 1
FEED_AHEAD = 4
PAIRS_AHEAD = 2
FEW = 2
MESH = pl.DeviceIdType.MESH


def fused_kernel(
    plan, held, latents, images,
    slot_ref, tok_ref, gate_ref, last_ref, first_ref, q_ref, k_ref, v_ref, out_ref, *scratch
):
    chunks = len(plan)
    starts = [sum(plan[:c]) * DH for c in range(chunks)]
    widths = [heads * DH for heads in plan]
    own, near, far, farthest, sel, q_all = (
        scratch[part * chunks : (part + 1) * chunks] for part in range(6)
    )
    (win, bias, own_sem, raw_send, raw_recv, rel_send, rel_recv,
     sel_send, sel_recv, q_sem, q_send, q_recv) = scratch[6 * chunks :]
    rows = q_ref.shape[0]
    half = q_ref.shape[1] // 2
    per_holder = MAXIMG // 4
    me = lax.axis_index("seq")
    mine = lax.axis_index("tensor")
    other = 1 - mine
    low = me < 2
    end = jnp.where(low, 0, 3)
    mid = jnp.where(low, 1, 2)
    far_mid = 3 - mid
    far_end = 3 - end
    is_end = me == end
    is_mid = me == mid
    peer = jnp.where(is_end, mid, far_mid)

    barrier = pltpu.get_barrier_semaphore()
    pl.semaphore_signal(barrier, inc=1, device_id={"tensor": other}, device_id_type=MESH)

    @pl.when(is_end)
    def _():
        pl.semaphore_signal(barrier, inc=1, device_id={"seq": mid}, device_id_type=MESH)
        pl.semaphore_wait(barrier, 2)

    @pl.when(is_mid)
    def _():
        pl.semaphore_signal(barrier, inc=1, device_id={"seq": end}, device_id_type=MESH)
        pl.semaphore_signal(barrier, inc=1, device_id={"seq": far_mid}, device_id_type=MESH)
        pl.semaphore_wait(barrier, 3)

    def cols(c):
        return pl.ds(starts[c], widths[c])

    def own_copy(c, kv):
        src = (k_ref, v_ref)[kv]
        return pltpu.make_async_copy(src.at[:, :, cols(c)], own[c].at[kv], own_sem.at[c, kv])

    def raw_copy(c, kv, frm, to):
        src = (k_ref, v_ref)[kv]
        which = 0 if frm is end else 1
        return pltpu.make_async_remote_copy(
            src_ref=src.at[:, :, cols(c)],
            dst_ref=(near, far)[which][c].at[kv],
            send_sem=raw_send.at[c, kv],
            recv_sem=raw_recv.at[which, c, kv],
            device_id={"seq": to},
            device_id_type=MESH,
        )

    def relay_copy(c):
        return pltpu.make_async_remote_copy(
            src_ref=near[c], dst_ref=farthest[c],
            send_sem=rel_send.at[c], recv_sem=rel_recv.at[c],
            device_id={"seq": far_mid}, device_id_type=MESH,
        )

    origins = (mid, far_mid, far_end)

    def sel_copy(c, n):
        return pltpu.make_async_remote_copy(
            src_ref=sel[c].at[:, pl.ds(n * per_holder, per_holder)],
            dst_ref=(near, far, farthest)[n][c].at[:, pl.ds(0, per_holder)],
            send_sem=sel_send.at[c, n],
            recv_sem=sel_recv.at[c, n],
            device_id={"seq": end},
            device_id_type=MESH,
        )

    def q_local(c):
        return pltpu.make_async_copy(
            q_ref.at[:, pl.ds(pl.multiple_of(mine * half + starts[c], DH), widths[c])],
            q_all[c].at[pl.ds(mine * rows, rows)],
            q_sem.at[c],
        )

    def q_remote(c):
        return pltpu.make_async_remote_copy(
            src_ref=q_ref.at[:, pl.ds(pl.multiple_of(other * half + starts[c], DH), widths[c])],
            dst_ref=q_all[c].at[pl.ds(mine * rows, rows)],
            send_sem=q_send.at[c],
            recv_sem=q_recv.at[c],
            device_id={"tensor": other},
            device_id_type=MESH,
        )

    def q_arrival(c):
        return pltpu.make_async_remote_copy(
            src_ref=q_all[c].at[pl.ds(other * rows, rows)],
            dst_ref=q_all[c].at[pl.ds(other * rows, rows)],
            send_sem=q_send.at[c],
            recv_sem=q_recv.at[c],
            device_id={"tensor": other},
            device_id_type=MESH,
        )

    @pl.when(is_end)
    def _():
        for c in range(chunks):
            for kv in range(2):
                raw_copy(c, kv, end, mid).start()

    @pl.when(is_mid)
    def _():
        for c in range(min(2, chunks)):
            for kv in range(2):
                raw_copy(c, kv, mid, far_mid).start()

    for c in range(chunks):
        q_remote(c).start()
    for c in range(chunks):
        for kv in range(2):
            own_copy(c, kv).start()
        q_local(c).start()

    base = jnp.where(
        me == 0, 0, jnp.where(me == 3, images - MAXIMG, jnp.minimum(tok_ref[0], images - MAXIMG))
    )
    neighbour = jnp.where(is_end, mid, end)
    window_rows = []
    for w in range(MAXIMG):
        row = slot_ref[base + w]
        owner = sum(jnp.where(row >= t * held, 1, 0) for t in range(1, 4))
        local = jnp.where(is_end & (owner != me), w // 4, row - owner * held)
        window_rows.append((owner, local))
    end_base = jnp.where(low, 0, images - MAXIMG)
    sel_rows = []
    for origin in origins:
        for k in range(per_holder):
            found = 0
            for t in range(4):
                row = slot_ref[end_base + 4 * k + t]
                inside = (row >= origin * held) & (row < (origin + 1) * held)
                found = found + jnp.where(inside, row - origin * held, 0)
            sel_rows.append(found)

    def send_selected(c, n):
        source = (own, far, farthest)[n][c]
        for at in range(n * per_holder, (n + 1) * per_holder):
            for kv in range(2):
                sel[c][kv, at] = source[kv, sel_rows[at]]
        sel_copy(c, n).start()

    def send_own(c):
        for kv in range(2):
            own_copy(c, kv).wait()
        send_selected(c, 0)

    def pick(c, kv, owner, local):
        image = own[c][kv, local]
        for part, holder in ((near, neighbour), (far, far_mid), (farthest, far_end)):
            image = jnp.where(owner == holder, part[c][kv, local], image)
        return image

    @pl.when(is_mid)
    def _():
        for c in range(LEAD):
            send_own(c)

    tokens = 2 * rows
    ids = base + lax.broadcasted_iota(jnp.int32, (1, MAXIMG * latents), 1) // latents
    for r in range(tokens // DH):
        last = jnp.transpose(jnp.broadcast_to(last_ref[r : r + 1, :], (DH, DH)))
        first = jnp.transpose(jnp.broadcast_to(first_ref[r : r + 1, :], (DH, DH)))
        for at in range(0, MAXIMG * latents, DH):
            part = ids[:, at : at + DH]
            bias[r * DH : (r + 1) * DH, at : at + DH] = jnp.where(
                (part >= first) & (part <= last), 0.0, -1e30
            )
    gates = jnp.tanh(gate_ref[...])
    factor = math.log2(math.e) / math.sqrt(DH)

    for s in range(chunks + 2):
        if s < chunks:
            @pl.when(is_mid)
            def _():
                for kv in range(2):
                    raw_copy(s, kv, end, mid).wait_recv()
                relay_copy(s).start()
                if s + 2 < chunks:
                    for kv in range(2):
                        raw_copy(s + 2, kv, mid, far_mid).start()
        if 0 <= s - 1 < chunks:
            c = s - 1

            @pl.when(is_mid)
            def _():
                for kv in range(2):
                    raw_copy(c, kv, far_mid, mid).wait_recv()
                send_selected(c, 1)
                relay_copy(c).wait_recv()
                send_selected(c, 2)
                if c + LEAD < chunks:
                    send_own(c + LEAD)

        if 0 <= s - 2 < chunks:
            c = s - 2

            @pl.when(is_end)
            def _():
                for kv in range(2):
                    own_copy(c, kv).wait()
                for n in range(3):
                    sel_copy(c, n).wait_recv()

            q_local(c).wait()
            q_arrival(c).wait_recv()
            for w in range(MAXIMG):
                for kv in range(2):
                    win[kv, w * latents : (w + 1) * latents, : widths[c]] = pick(c, kv, *window_rows[w])

            def attend(i, carry):
                at = pl.ds(i * TILE, TILE)
                for h in range(plan[c]):
                    lane = slice(h * DH, (h + 1) * DH)
                    scores = lax.dot_general(
                        q_all[c][at, lane], win[0, :, lane], (((1,), (1,)), ((), ())),
                        preferred_element_type=jnp.float32,
                    ) + bias[at, :]
                    top = jnp.max(scores, axis=1, keepdims=True)
                    raised = jnp.exp2((scores - top) * factor)
                    total = jnp.sum(raised, axis=1, keepdims=True)
                    summed = jnp.dot(
                        raised.astype(jnp.bfloat16), win[1, :, lane],
                        preferred_element_type=jnp.float32,
                    )
                    at_col = starts[c] + h * DH
                    gate = gates[:, at_col // DH : at_col // DH + 1]
                    out_ref[at, at_col : at_col + DH] = (summed * (gate / total)).astype(
                        jnp.bfloat16
                    )
                return carry

            lax.fori_loop(0, tokens // TILE, attend, 0)

    for c in range(chunks):
        q_remote(c).wait_send()

    @pl.when(is_end)
    def _():
        for c in range(chunks):
            for kv in range(2):
                raw_copy(c, kv, end, mid).wait_send()

    @pl.when(is_mid)
    def _():
        for c in range(chunks):
            for kv in range(2):
                raw_copy(c, kv, mid, far_mid).wait_send()
            relay_copy(c).wait_send()
            for n in range(3):
                sel_copy(c, n).wait_send()


def fused(queries, image_keys, image_values, head_gate, token_image, span_first, image_slot):
    rows, _, all_width = queries.shape
    held, latents, _, head_width = image_keys.shape
    images = image_slot.shape[0]
    heads = head_width // DH
    plan = (1, 1) + (2,) * ((heads - 4) // 2) + (1, 1)
    chunks = len(plan)
    widths = [count * DH for count in plan]
    smem = pl.BlockSpec(memory_space=pltpu.SMEM)
    vmem = pl.BlockSpec(memory_space=pltpu.VMEM)
    hbm = pl.BlockSpec(memory_space=pl.ANY)
    dma = pltpu.SemaphoreType.DMA
    out = pl.pallas_call(
        functools.partial(fused_kernel, plan, held, latents, images),
        out_shape=jax.ShapeDtypeStruct((2 * rows, head_width), jnp.bfloat16),
        in_specs=[smem, smem, vmem, vmem, vmem, hbm, hbm, hbm],
        out_specs=vmem,
        scratch_shapes=[pltpu.VMEM((2, held, latents, width), jnp.bfloat16) for width in widths * 4]
        + [pltpu.VMEM((2, 3 * MAXIMG // 4, latents, width), jnp.bfloat16) for width in widths]
        + [pltpu.VMEM((2 * rows, width), jnp.bfloat16) for width in widths]
        + [
            pltpu.VMEM((2, MAXIMG * latents, max(widths)), jnp.bfloat16),
            pltpu.VMEM((2 * rows, MAXIMG * latents), jnp.float32),
            dma((chunks, 2)),
            dma((chunks, 2)),
            dma((2, chunks, 2)),
            dma((chunks,)),
            dma((chunks,)),
            dma((chunks, 3)),
            dma((chunks, 3)),
            dma((chunks,)),
            dma((chunks,)),
            dma((chunks,)),
        ],
        compiler_params=pltpu.CompilerParams(
            collective_id=0, has_side_effects=True, vmem_limit_bytes=36 * 1024 * 1024
        ),
    )(
        image_slot,
        token_image,
        head_gate,
        token_image.reshape(-1, DH),
        span_first.reshape(-1, DH),
        queries.reshape(rows, all_width),
        image_keys.reshape(held, latents, head_width),
        image_values.reshape(held, latents, head_width),
    )
    return out


def offloaded(head):
    return head % 2 == 0


def split_kernel(
    heads, held, latents, images, few,
    slot_ref, gate_ref, last_ref, first_ref, q_ref, k_ref, v_ref, out_ref, flag_ref, *scratch
):
    own, near, far, q_all, q_end = (scratch[part * heads : (part + 1) * heads] for part in range(5))
    (across, toward, results, win, bias, marks, marks_all, flag_out, flag_in,
     mark_send, mark_recv, mark_sem, flag_sem, own_sem, raw_send, raw_recv, x_send, x_recv,
     y_send, y_recv, q_sem, q_send, q_recv, qe_send, qe_recv, o_send, o_recv) = scratch[5 * heads :]
    rows = q_ref.shape[0]
    tokens = 2 * rows
    half = q_ref.shape[1] // 2
    tiles = tokens // TILE
    per_holder = MAXIMG // 4
    big_slots = 2 * per_holder
    me = lax.axis_index("seq")
    mine = lax.axis_index("tensor")
    other = 1 - mine
    group = lax.axis_index("groups")
    low = me < 2
    end = jnp.where(low, 0, 3)
    mid = jnp.where(low, 1, 2)
    far_mid = 3 - mid
    far_end = 3 - end
    is_end = me == end
    is_mid = me == mid
    peers = [lax.rem(me + d, 4) for d in range(1, 4)]

    barrier = pltpu.get_barrier_semaphore()
    pl.semaphore_signal(barrier, inc=1, device_id={"tensor": other}, device_id_type=MESH)
    pl.semaphore_signal(barrier, inc=1, device_id={"groups": 1 - group}, device_id_type=MESH)
    for peer in peers:
        pl.semaphore_signal(barrier, inc=1, device_id={"seq": peer}, device_id_type=MESH)
    marks_all[me, 0:8] = last_ref[...]
    marks_all[me, 8:16] = first_ref[...]
    pl.semaphore_wait(barrier, 5)

    def remote(src, dst, send, recv, **to):
        return pltpu.make_async_remote_copy(
            src_ref=src, dst_ref=dst, send_sem=send, recv_sem=recv, device_id=to, device_id_type=MESH
        )

    def mark_copy(d, row, to):
        return remote(
            marks_all.at[row], marks_all.at[row], mark_send.at[d], mark_recv.at[row], seq=to
        )

    def cols(c):
        return pl.ds(c * DH, DH)

    def own_copy(c, kv):
        return pltpu.make_async_copy((k_ref, v_ref)[kv].at[:, :, cols(c)], own[c].at[kv], own_sem.at[c, kv])

    def raw_copy(c, kv):
        src = (k_ref, v_ref)[kv].at[:, :, cols(c)]
        return remote(src, near[c].at[kv], raw_send.at[c, kv], raw_recv.at[c, kv], seq=mid)

    def cross_copy(c, part):
        at = pl.ds(0, per_holder) if part == 0 else pl.ds(per_holder, per_holder + few)
        return remote(
            across.at[c, :, at], far[c].at[:, at], x_send.at[c, part], x_recv.at[c, part], seq=far_mid
        )

    def toward_copy(c, part):
        first, second = pl.ds(0, per_holder), pl.ds(per_holder, per_holder)
        src, dst = (
            (toward.at[c // 2, :, first], near[c].at[:, first]),
            (far[c].at[:, first], far[c].at[:, first]),
            (toward.at[c // 2, :, second], far[c].at[:, second]),
        )[part]
        return remote(src, dst, y_send.at[c, part], y_recv.at[c, part], seq=end)

    def q_cols(who, c):
        return pl.ds(pl.multiple_of(who * half + c * DH, DH), DH)

    def q_local(c):
        return pltpu.make_async_copy(
            q_ref.at[:, q_cols(mine, c)], q_all[c].at[pl.ds(mine * rows, rows)], q_sem.at[c]
        )

    def q_remote(c):
        return remote(
            q_ref.at[:, q_cols(other, c)], q_all[c].at[pl.ds(mine * rows, rows)],
            q_send.at[c], q_recv.at[c], tensor=other,
        )

    def q_arrival(c):
        landed = q_all[c].at[pl.ds(other * rows, rows)]
        return remote(landed, landed, q_send.at[c], q_recv.at[c], tensor=other)

    def q_lend(c, part):
        who = (mine, other)[part]
        at = pl.ds(who * rows, rows)
        src = q_ref.at[:, q_cols(mine, c)] if part == 0 else q_all[c].at[at]
        return remote(src, q_end[c].at[at], qe_send.at[c // 2, part], qe_recv.at[c // 2, part], seq=mid)

    def result_copy(c, i):
        at = pl.ds(i * TILE, TILE)
        return remote(
            results.at[c // 2, at], results.at[c // 2, at],
            o_send.at[c // 2, i], o_recv.at[c // 2, i], seq=end,
        )

    def send_pair(p):
        for c in (2 * p, 2 * p + 1):
            for kv in range(2):
                raw_copy(c, kv).start()
        q_lend(2 * p, 0).start()
        q_arrival(2 * p).wait_recv()
        q_lend(2 * p, 1).start()

    for d in range(3):
        mark_copy(d, me, peers[d]).start()
    q_remote(0).start()

    @pl.when(is_end)
    def _():
        for c in (0, 1):
            for kv in range(2):
                raw_copy(c, kv).start()
        q_lend(0, 0).start()

    for c in range(1, heads):
        q_remote(c).start()

    @pl.when(is_end)
    def _():
        q_arrival(0).wait_recv()
        q_lend(0, 1).start()
        for p in range(1, PAIRS_AHEAD):
            send_pair(p)
        for c in range(heads):
            if not offloaded(c):
                for kv in range(2):
                    own_copy(c, kv).start()
                q_local(c).start()

    @pl.when(is_mid)
    def _():
        for c in range(heads):
            for kv in range(2):
                own_copy(c, kv).start()
        for c in range(heads):
            q_local(c).start()

    for d in range(3):
        mark_copy(d, peers[d], peers[d]).wait_recv()
    fetch = pltpu.make_async_copy(marks_all, marks, mark_sem)
    fetch.start()
    fetch.wait()

    def owner_of(row):
        return sum(jnp.where(row >= t * held, 1, 0) for t in range(1, 4))

    slots = [slot_ref[j] for j in range(images)]
    owners = [owner_of(row) for row in slots]

    def base_of(i):
        return jnp.minimum(marks[i, 0, 0], images - MAXIMG)

    def side_plan(left):
        one = jnp.where(left, 0, 2)
        spans = []
        for i in (one, one + 1):
            spans.append((jnp.maximum(base_of(i), marks[i, 8, 0]), marks[i, 7, DH - 1]))
        one_big = spans[0][1] - spans[0][0] >= spans[1][1] - spans[1][0]
        big = jnp.where(one_big, one, one + 1)
        lo = jnp.where(one_big, spans[1][0], spans[0][0])
        hi = jnp.where(one_big, spans[1][1], spans[0][1])
        count = 0
        ids = [0] * few
        for j in range(images):
            away = (owners[j] >= 2) == left
            hit = (j >= lo) & (j <= hi) & away
            ids = [jnp.where(hit & (count == n), j, ids[n]) for n in range(few)]
            count = count + jnp.where(hit, 1, 0)
        return big, ids, count

    here_big, here_ids, here_count = side_plan(low)
    there_big, there_ids, there_count = side_plan(jnp.logical_not(low))
    bad = jnp.where((here_count > few) | (there_count > few), 1, 0)
    flag_out[...] = jnp.zeros(flag_out.shape, jnp.int32) + bad
    flag_copy = remote(flag_out, flag_in, flag_sem.at[0], flag_sem.at[1], groups=1 - group)
    flag_copy.start()

    def held_rows(base, origin):
        found_rows = []
        for k in range(per_holder):
            found = 0
            for t in range(4):
                row = slot_ref[base + 4 * k + t]
                inside = (row >= origin * held) & (row < (origin + 1) * held)
                found = found + jnp.where(inside, row - origin * held, 0)
            found_rows.append(jnp.minimum(found, held - 1))
        return found_rows

    def window(i, at_end):
        base = base_of(i)
        is_big = here_big == i
        places = []
        for w in range(MAXIMG):
            row = slot_ref[base + w]
            owner = owner_of(row)
            local = row - owner * held
            away = (owner >= 2) == low
            slot = 0
            for n in range(few - 1, -1, -1):
                slot = jnp.where(here_ids[n] == base + w, n, slot)
            fewer = jnp.where(at_end, per_holder + lax.rem(slot, per_holder), big_slots + slot)
            place = jnp.where(is_big, jnp.where(owner == far_mid, 0, per_holder) + w // 4, fewer)
            beside = jnp.where(at_end, w // 4, local)
            source = jnp.where(away, 2, jnp.where(owner == me, 0, 1))
            places.append((
                source,
                jnp.where(source == 0, local, 0),
                jnp.where(source == 1, beside, 0),
                jnp.where(source == 2, place, 0),
            ))
        return places

    there_base = base_of(there_big)
    big_mine = held_rows(there_base, me)
    big_near = held_rows(there_base, end)
    end_mine = held_rows(base_of(end), me)
    few_rows = []
    for n in range(few):
        row = slot_ref[there_ids[n]]
        owner = owner_of(row)
        few_rows.append((owner == me, row - owner * held))
    end_far = [
        jnp.where(here_big == end, per_holder + j, big_slots + j % few) for j in range(per_holder)
    ]

    def lend_own(c):
        for k in range(per_holder):
            for kv in range(2):
                across[c, kv, k] = own[c][kv, big_mine[k]]
        cross_copy(c, 0).start()

    def lend_near(c):
        for k in range(per_holder):
            for kv in range(2):
                across[c, kv, per_holder + k] = near[c][kv, big_near[k]]
        for n in range(few):
            is_own, row = few_rows[n]
            for kv in range(2):
                across[c, kv, big_slots + n] = jnp.where(is_own, own[c][kv, row], near[c][kv, row])
        cross_copy(c, 1).start()

    def feed_own(c):
        for k in range(per_holder):
            for kv in range(2):
                toward[c // 2, kv, k] = own[c][kv, end_mine[k]]
        toward_copy(c, 0).start()

    def feed_far(c):
        for j in range(per_holder):
            for kv in range(2):
                toward[c // 2, kv, per_holder + j] = far[c][kv, end_far[j]]
        toward_copy(c, 2).start()

    own_waited = set()

    def need_own(c):
        if c not in own_waited:
            own_waited.add(c)
            for kv in range(2):
                own_copy(c, kv).wait()

    @pl.when(is_mid)
    def _():
        for c in range(max(AHEAD, FEED_AHEAD)):
            need_own(c)
            if c < AHEAD:
                lend_own(c)
            if c < FEED_AHEAD and not offloaded(c):
                feed_own(c)

    def fill_bias(which, i):
        ids = base_of(i) + lax.broadcasted_iota(jnp.int32, (1, MAXIMG * latents), 1) // latents
        for r in range(tokens // DH):
            last = jnp.transpose(jnp.broadcast_to(marks_all[i, r : r + 1, :], (DH, DH)))
            first = jnp.transpose(jnp.broadcast_to(marks_all[i, 8 + r : 9 + r, :], (DH, DH)))
            for at in range(0, MAXIMG * latents, DH):
                part = ids[:, at : at + DH]
                bias[which, r * DH : (r + 1) * DH, at : at + DH] = jnp.where(
                    (part >= first) & (part <= last), 0.0, -1e30
                )

    my_window = window(me, is_end)
    end_window = window(end, False)
    fill_bias(0, me)

    @pl.when(is_mid)
    def _():
        fill_bias(1, end)

    gates = jnp.tanh(gate_ref[...])
    factor = math.log2(math.e) / math.sqrt(DH)

    def fill_window(which, c, places):
        for w in range(MAXIMG):
            source, own_row, near_row, far_row = places[w]
            for kv in range(2):
                image = jnp.where(source == 1, near[c][kv, near_row], own[c][kv, own_row])
                win[which, kv, w * latents : (w + 1) * latents] = jnp.where(
                    source == 2, far[c][kv, far_row], image
                )

    def attend(which, q, c, store):
        gate = gates[:, c : c + 1]

        def tile(i, carry):
            at = pl.ds(pl.multiple_of(i * TILE, TILE), TILE)
            scores = lax.dot_general(
                q[at, :], win[which, 0], (((1,), (1,)), ((), ())), preferred_element_type=jnp.float32
            ) + bias[which, at, :]
            top = jnp.max(scores, axis=1, keepdims=True)
            raised = jnp.exp2((scores - top) * factor)
            total = jnp.sum(raised, axis=1, keepdims=True)
            summed = jnp.dot(
                raised.astype(jnp.bfloat16), win[which, 1], preferred_element_type=jnp.float32
            )
            store(i, at, (summed * (gate / total)).astype(jnp.bfloat16))
            return carry

        lax.fori_loop(0, tiles, tile, 0)

    def own_head(c):
        q_local(c).wait()
        q_arrival(c).wait_recv()
        fill_window(0, c, my_window)

        def store(i, at, value):
            out_ref[at, c * DH : (c + 1) * DH] = value

        attend(0, q_all[c], c, store)

    def end_head(c):
        for part in range(2):
            q_lend(c, part).wait_recv()
        fill_window(1, c, end_window)

        def store(i, at, value):
            results[c // 2, at, :] = value
            result_copy(c, i).start()

        attend(1, q_end[c], c, store)

    for s in range(heads + 2):
        c = s - 1
        lent = s - 3

        @pl.when(is_mid)
        def _():
            if s < heads:
                for kv in range(2):
                    raw_copy(s, kv).wait_recv()
                lend_near(s)
                if s + AHEAD < heads:
                    need_own(s + AHEAD)
                    lend_own(s + AHEAD)
                ahead = s + FEED_AHEAD
                if ahead < heads and not offloaded(ahead):
                    need_own(ahead)
                    feed_own(ahead)
                cross_copy(s, 0).wait_recv()
                if not offloaded(s):
                    toward_copy(s, 1).start()
            if 0 <= c < heads:
                cross_copy(c, 1).wait_recv()
                if offloaded(c):
                    own_head(c)
                else:
                    feed_far(c)
            if c == heads - 1:
                end_head(heads - 2)

        if 0 <= c < heads and not offloaded(c):
            @pl.when(is_end)
            def _():
                if c // 2 + PAIRS_AHEAD < heads // 2:
                    send_pair(c // 2 + PAIRS_AHEAD)
                for kv in range(2):
                    own_copy(c, kv).wait()
                for part in range(3):
                    toward_copy(c, part).wait_recv()

            own_head(c)

        if 0 <= lent < heads and offloaded(lent):
            if lent < heads - 2:
                @pl.when(is_mid)
                def _():
                    end_head(lent)

            @pl.when(is_end)
            def _():
                for i in range(tiles):
                    result_copy(lent, i).wait_recv()
                out_ref[:, lent * DH : (lent + 1) * DH] = results[lent // 2]

    flag_copy.wait()
    flag_ref[...] = jnp.maximum(flag_out[...], flag_in[...])
    for d in range(3):
        mark_copy(d, me, peers[d]).wait_send()
    for c in range(heads):
        q_remote(c).wait_send()

    @pl.when(is_end)
    def _():
        for c in range(heads):
            for kv in range(2):
                raw_copy(c, kv).wait_send()
            if offloaded(c):
                for part in range(2):
                    q_lend(c, part).wait_send()

    @pl.when(is_mid)
    def _():
        for c in range(heads):
            for part in range(2):
                cross_copy(c, part).wait_send()
            if offloaded(c):
                for i in range(tiles):
                    result_copy(c, i).wait_send()
            else:
                for part in range(3):
                    toward_copy(c, part).wait_send()


def split(queries, image_keys, image_values, head_gate, token_image, span_first, image_slot):
    rows, _, all_width = queries.shape
    held, latents, _, head_width = image_keys.shape
    images = image_slot.shape[0]
    heads = head_width // DH
    tokens = 2 * rows
    tiles = tokens // TILE
    slots = MAXIMG // 2 + FEW
    smem = pl.BlockSpec(memory_space=pltpu.SMEM)
    vmem = pl.BlockSpec(memory_space=pltpu.VMEM)
    hbm = pl.BlockSpec(memory_space=pl.ANY)
    dma = pltpu.SemaphoreType.DMA
    bf16 = jnp.bfloat16
    return pl.pallas_call(
        functools.partial(split_kernel, heads, held, latents, images, FEW),
        out_shape=(pltpu.VMEM((tokens, head_width), bf16), jax.ShapeDtypeStruct((8, DH), jnp.int32)),
        in_specs=[smem, vmem, vmem, vmem, hbm, hbm, hbm],
        out_specs=(vmem, vmem),
        scratch_shapes=[pltpu.VMEM((2, held, latents, DH), bf16)] * (2 * heads)
        + [pltpu.VMEM((2, slots, latents, DH), bf16)] * heads
        + [pltpu.VMEM((tokens, DH), bf16)] * heads
        + [pltpu.VMEM((tokens if offloaded(c) else 16, DH), bf16) for c in range(heads)]
        + [
            pltpu.VMEM((heads, 2, slots, latents, DH), bf16),
            pltpu.VMEM((heads // 2, 2, MAXIMG // 2, latents, DH), bf16),
            pltpu.VMEM((heads // 2, tokens, DH), bf16),
            pltpu.VMEM((2, 2, MAXIMG * latents, DH), bf16),
            pltpu.VMEM((2, tokens, MAXIMG * latents), jnp.float32),
            pltpu.SMEM((4, 16, DH), jnp.int32),
            pltpu.VMEM((4, 16, DH), jnp.int32),
            pltpu.VMEM((8, DH), jnp.int32),
            pltpu.VMEM((8, DH), jnp.int32),
            dma((3,)),
            dma((4,)),
            dma,
            dma((2,)),
            dma((heads, 2)),
            dma((heads, 2)),
            dma((heads, 2)),
            dma((heads, 2)),
            dma((heads, 2)),
            dma((heads, 3)),
            dma((heads, 3)),
            dma((heads,)),
            dma((heads,)),
            dma((heads,)),
            dma((heads // 2, 2)),
            dma((heads // 2, 2)),
            dma((heads // 2, tiles)),
            dma((heads // 2, tiles)),
        ],
        compiler_params=pltpu.CompilerParams(
            collective_id=1, has_side_effects=True, vmem_limit_bytes=40 * 1024 * 1024
        ),
    )(
        image_slot,
        head_gate,
        token_image.reshape(-1, DH),
        span_first.reshape(-1, DH),
        queries.reshape(rows, all_width),
        image_keys.reshape(held, latents, head_width),
        image_values.reshape(held, latents, head_width),
    )


def attended(*args):
    result, flag = split(*args)
    bad = flag[0, 0]
    kept = jnp.where(args[4][0] < 0, jnp.bfloat16(0), result)
    result = lax.while_loop(
        lambda c: c[0] > 0, lambda c: (0, jnp.where(c[0] > 0, fused(*args), c[1])), (bad, kept)
    )[1]
    return result.reshape(result.shape[0], 1, result.shape[1])


def lookup(lookup_table, at_index):
    count = lookup_table.shape[0]
    hits = jnp.arange(count, dtype=jnp.int32) == at_index[..., None]
    return jnp.sum(jnp.where(hits, lookup_table, 0), axis=-1)


def per_device(queries, image_keys, image_values, head_gate, token_image, span_first, image_slot):
    tensor_count = lax.axis_size("tensor")
    row_count = queries.shape[0]
    half_width = queries.shape[2]
    split_rows = queries.reshape(row_count, tensor_count, half_width // tensor_count)
    head_rows = lax.all_to_all(split_rows, "tensor", split_axis=1, concat_axis=0, tiled=True)
    token_count = head_rows.shape[0]
    head_width = head_rows.shape[2]
    head_count = head_width // DH
    held_count = image_keys.shape[0]
    latents = image_keys.shape[1]
    images = image_slot.shape[0]
    packed = jnp.concatenate([image_keys[:, :, 0, :], image_values[:, :, 0, :]], axis=2)
    packed = packed.reshape(held_count, latents * 2 * head_width)
    window_start = jnp.minimum(token_image[0], images - MAXIMG)
    window_ids = window_start + jnp.arange(MAXIMG, dtype=jnp.int32)
    in_window = window_ids < images
    safe_ids = jnp.minimum(window_ids, images - 1)
    window_slot = lookup(image_slot, safe_ids)
    fragment = lax.all_gather(packed, "seq", axis=0, tiled=True)
    piece_rows = jnp.arange(fragment.shape[0], dtype=jnp.int32)
    select = ((window_slot[:, None] == piece_rows[None, :]) & in_window[:, None]).astype(
        jnp.bfloat16
    )
    window = jnp.dot(select, fragment, preferred_element_type=jnp.float32).astype(jnp.bfloat16)
    window = window.reshape(MAXIMG * latents, 2 * head_width)
    keys_win = window[:, :head_width]
    values_win = window[:, head_width:]
    visible = (window_ids[None, :] >= span_first[:, None]) & (
        window_ids[None, :] <= token_image[:, None]
    )
    key_mask = jnp.repeat(visible, latents, axis=1)
    score_scale = 1.0 / math.sqrt(DH)
    gate_values = jnp.tanh(head_gate.reshape(-1))
    results = []
    for head_index in range(head_count):
        low_col = head_index * DH
        head_query = head_rows[:, 0, low_col : low_col + DH]
        scores = (
            lax.dot_general(
                head_query,
                keys_win[:, low_col : low_col + DH],
                (((1,), (1,)), ((), ())),
                preferred_element_type=jnp.float32,
            )
            * score_scale
        )
        row_top = jnp.max(jnp.where(key_mask, scores, -1e30), axis=1, keepdims=True)
        raised = jnp.exp(jnp.where(key_mask, scores - row_top, -1e30))
        row_total = jnp.sum(raised, axis=1, keepdims=True)
        weights = raised.astype(jnp.bfloat16)
        summed = jnp.dot(
            weights, values_win[:, low_col : low_col + DH], preferred_element_type=jnp.float32
        )
        results.append(summed / row_total * gate_values[head_index])
    attended = jnp.concatenate(results, axis=1).astype(jnp.bfloat16)
    return attended.reshape(token_count, 1, head_width)


def solution(mesh):
    placed = (
        P(("groups", "seq", "tensor"), "sub", None),
        P(("groups", "seq"), None, "sub", "tensor"),
        P(("groups", "seq"), None, "sub", "tensor"),
        P("sub", "tensor"),
        P(("groups", "seq")),
        P(("groups", "seq")),
        P("groups"),
    )
    fits = mesh.shape["seq"] == 4 and mesh.shape["tensor"] == 2
    return jax.shard_map(
        attended if fits else per_device,
        mesh=mesh,
        in_specs=placed,
        out_specs=P(("groups", "seq"), "sub", "tensor"),
        check_vma=False,
    )
```

```python
import functools
import math

import jax
import jax.numpy as jnp
from jax import lax
from jax.experimental import pallas as pl
from jax.experimental.pallas import tpu as pltpu
from jax.sharding import PartitionSpec as P

DH = 128
MAXIMG = 16
TILE = 256
LEAD = 3
AHEAD = 2
FEED_AHEAD = 8
PAIRS_AHEAD = 3
FEW = 2
MESH = pl.DeviceIdType.MESH


def fused_kernel(
    plan, held, latents, images,
    slot_ref, tok_ref, gate_ref, last_ref, first_ref, q_ref, k_ref, v_ref, out_ref, *scratch
):
    chunks = len(plan)
    starts = [sum(plan[:c]) * DH for c in range(chunks)]
    widths = [heads * DH for heads in plan]
    own, near, far, farthest, sel, q_all = (
        scratch[part * chunks : (part + 1) * chunks] for part in range(6)
    )
    (win, bias, own_sem, raw_send, raw_recv, rel_send, rel_recv,
     sel_send, sel_recv, q_sem, q_send, q_recv) = scratch[6 * chunks :]
    rows = q_ref.shape[0]
    half = q_ref.shape[1] // 2
    per_holder = MAXIMG // 4
    me = lax.axis_index("seq")
    mine = lax.axis_index("tensor")
    other = 1 - mine
    low = me < 2
    end = jnp.where(low, 0, 3)
    mid = jnp.where(low, 1, 2)
    far_mid = 3 - mid
    far_end = 3 - end
    is_end = me == end
    is_mid = me == mid
    peer = jnp.where(is_end, mid, far_mid)

    barrier = pltpu.get_barrier_semaphore()
    pl.semaphore_signal(barrier, inc=1, device_id={"tensor": other}, device_id_type=MESH)

    @pl.when(is_end)
    def _():
        pl.semaphore_signal(barrier, inc=1, device_id={"seq": mid}, device_id_type=MESH)
        pl.semaphore_wait(barrier, 2)

    @pl.when(is_mid)
    def _():
        pl.semaphore_signal(barrier, inc=1, device_id={"seq": end}, device_id_type=MESH)
        pl.semaphore_signal(barrier, inc=1, device_id={"seq": far_mid}, device_id_type=MESH)
        pl.semaphore_wait(barrier, 3)

    def cols(c):
        return pl.ds(starts[c], widths[c])

    def own_copy(c, kv):
        src = (k_ref, v_ref)[kv]
        return pltpu.make_async_copy(src.at[:, :, cols(c)], own[c].at[kv], own_sem.at[c, kv])

    def raw_copy(c, kv, frm, to):
        src = (k_ref, v_ref)[kv]
        which = 0 if frm is end else 1
        return pltpu.make_async_remote_copy(
            src_ref=src.at[:, :, cols(c)],
            dst_ref=(near, far)[which][c].at[kv],
            send_sem=raw_send.at[c, kv],
            recv_sem=raw_recv.at[which, c, kv],
            device_id={"seq": to},
            device_id_type=MESH,
        )

    def relay_copy(c):
        return pltpu.make_async_remote_copy(
            src_ref=near[c], dst_ref=farthest[c],
            send_sem=rel_send.at[c], recv_sem=rel_recv.at[c],
            device_id={"seq": far_mid}, device_id_type=MESH,
        )

    origins = (mid, far_mid, far_end)

    def sel_copy(c, n):
        return pltpu.make_async_remote_copy(
            src_ref=sel[c].at[:, pl.ds(n * per_holder, per_holder)],
            dst_ref=(near, far, farthest)[n][c].at[:, pl.ds(0, per_holder)],
            send_sem=sel_send.at[c, n],
            recv_sem=sel_recv.at[c, n],
            device_id={"seq": end},
            device_id_type=MESH,
        )

    def q_local(c):
        return pltpu.make_async_copy(
            q_ref.at[:, pl.ds(pl.multiple_of(mine * half + starts[c], DH), widths[c])],
            q_all[c].at[pl.ds(mine * rows, rows)],
            q_sem.at[c],
        )

    def q_remote(c):
        return pltpu.make_async_remote_copy(
            src_ref=q_ref.at[:, pl.ds(pl.multiple_of(other * half + starts[c], DH), widths[c])],
            dst_ref=q_all[c].at[pl.ds(mine * rows, rows)],
            send_sem=q_send.at[c],
            recv_sem=q_recv.at[c],
            device_id={"tensor": other},
            device_id_type=MESH,
        )

    def q_arrival(c):
        return pltpu.make_async_remote_copy(
            src_ref=q_all[c].at[pl.ds(other * rows, rows)],
            dst_ref=q_all[c].at[pl.ds(other * rows, rows)],
            send_sem=q_send.at[c],
            recv_sem=q_recv.at[c],
            device_id={"tensor": other},
            device_id_type=MESH,
        )

    @pl.when(is_end)
    def _():
        for c in range(chunks):
            for kv in range(2):
                raw_copy(c, kv, end, mid).start()

    @pl.when(is_mid)
    def _():
        for c in range(min(2, chunks)):
            for kv in range(2):
                raw_copy(c, kv, mid, far_mid).start()

    for c in range(chunks):
        q_remote(c).start()
    for c in range(chunks):
        for kv in range(2):
            own_copy(c, kv).start()
        q_local(c).start()

    base = jnp.where(
        me == 0, 0, jnp.where(me == 3, images - MAXIMG, jnp.minimum(tok_ref[0], images - MAXIMG))
    )
    neighbour = jnp.where(is_end, mid, end)
    window_rows = []
    for w in range(MAXIMG):
        row = slot_ref[base + w]
        owner = sum(jnp.where(row >= t * held, 1, 0) for t in range(1, 4))
        local = jnp.where(is_end & (owner != me), w // 4, row - owner * held)
        window_rows.append((owner, local))
    end_base = jnp.where(low, 0, images - MAXIMG)
    sel_rows = []
    for origin in origins:
        for k in range(per_holder):
            found = 0
            for t in range(4):
                row = slot_ref[end_base + 4 * k + t]
                inside = (row >= origin * held) & (row < (origin + 1) * held)
                found = found + jnp.where(inside, row - origin * held, 0)
            sel_rows.append(found)

    def send_selected(c, n):
        source = (own, far, farthest)[n][c]
        for at in range(n * per_holder, (n + 1) * per_holder):
            for kv in range(2):
                sel[c][kv, at] = source[kv, sel_rows[at]]
        sel_copy(c, n).start()

    def send_own(c):
        for kv in range(2):
            own_copy(c, kv).wait()
        send_selected(c, 0)

    def pick(c, kv, owner, local):
        image = own[c][kv, local]
        for part, holder in ((near, neighbour), (far, far_mid), (farthest, far_end)):
            image = jnp.where(owner == holder, part[c][kv, local], image)
        return image

    @pl.when(is_mid)
    def _():
        for c in range(LEAD):
            send_own(c)

    tokens = 2 * rows
    ids = base + lax.broadcasted_iota(jnp.int32, (1, MAXIMG * latents), 1) // latents
    for r in range(tokens // DH):
        last = jnp.transpose(jnp.broadcast_to(last_ref[r : r + 1, :], (DH, DH)))
        first = jnp.transpose(jnp.broadcast_to(first_ref[r : r + 1, :], (DH, DH)))
        for at in range(0, MAXIMG * latents, DH):
            part = ids[:, at : at + DH]
            bias[r * DH : (r + 1) * DH, at : at + DH] = jnp.where(
                (part >= first) & (part <= last), 0.0, -1e30
            )
    gates = jnp.tanh(gate_ref[...])
    factor = math.log2(math.e) / math.sqrt(DH)

    for s in range(chunks + 2):
        if s < chunks:
            @pl.when(is_mid)
            def _():
                for kv in range(2):
                    raw_copy(s, kv, end, mid).wait_recv()
                relay_copy(s).start()
                if s + 2 < chunks:
                    for kv in range(2):
                        raw_copy(s + 2, kv, mid, far_mid).start()
        if 0 <= s - 1 < chunks:
            c = s - 1

            @pl.when(is_mid)
            def _():
                for kv in range(2):
                    raw_copy(c, kv, far_mid, mid).wait_recv()
                send_selected(c, 1)
                relay_copy(c).wait_recv()
                send_selected(c, 2)
                if c + LEAD < chunks:
                    send_own(c + LEAD)

        if 0 <= s - 2 < chunks:
            c = s - 2

            @pl.when(is_end)
            def _():
                for kv in range(2):
                    own_copy(c, kv).wait()
                for n in range(3):
                    sel_copy(c, n).wait_recv()

            q_local(c).wait()
            q_arrival(c).wait_recv()
            for w in range(MAXIMG):
                for kv in range(2):
                    win[kv, w * latents : (w + 1) * latents, : widths[c]] = pick(c, kv, *window_rows[w])

            def attend(i, carry):
                at = pl.ds(i * TILE, TILE)
                for h in range(plan[c]):
                    lane = slice(h * DH, (h + 1) * DH)
                    scores = lax.dot_general(
                        q_all[c][at, lane], win[0, :, lane], (((1,), (1,)), ((), ())),
                        preferred_element_type=jnp.float32,
                    ) + bias[at, :]
                    top = jnp.max(scores, axis=1, keepdims=True)
                    raised = jnp.exp2((scores - top) * factor)
                    total = jnp.sum(raised, axis=1, keepdims=True)
                    summed = jnp.dot(
                        raised.astype(jnp.bfloat16), win[1, :, lane],
                        preferred_element_type=jnp.float32,
                    )
                    at_col = starts[c] + h * DH
                    gate = gates[:, at_col // DH : at_col // DH + 1]
                    out_ref[at, at_col : at_col + DH] = (summed * (gate / total)).astype(
                        jnp.bfloat16
                    )
                return carry

            lax.fori_loop(0, tokens // TILE, attend, 0)

    for c in range(chunks):
        q_remote(c).wait_send()

    @pl.when(is_end)
    def _():
        for c in range(chunks):
            for kv in range(2):
                raw_copy(c, kv, end, mid).wait_send()

    @pl.when(is_mid)
    def _():
        for c in range(chunks):
            for kv in range(2):
                raw_copy(c, kv, mid, far_mid).wait_send()
            relay_copy(c).wait_send()
            for n in range(3):
                sel_copy(c, n).wait_send()


def fused(queries, image_keys, image_values, head_gate, token_image, span_first, image_slot):
    rows, _, all_width = queries.shape
    held, latents, _, head_width = image_keys.shape
    images = image_slot.shape[0]
    heads = head_width // DH
    plan = (1, 1) + (2,) * ((heads - 4) // 2) + (1, 1)
    chunks = len(plan)
    widths = [count * DH for count in plan]
    smem = pl.BlockSpec(memory_space=pltpu.SMEM)
    vmem = pl.BlockSpec(memory_space=pltpu.VMEM)
    hbm = pl.BlockSpec(memory_space=pl.ANY)
    dma = pltpu.SemaphoreType.DMA
    out = pl.pallas_call(
        functools.partial(fused_kernel, plan, held, latents, images),
        out_shape=jax.ShapeDtypeStruct((2 * rows, head_width), jnp.bfloat16),
        in_specs=[smem, smem, vmem, vmem, vmem, hbm, hbm, hbm],
        out_specs=vmem,
        scratch_shapes=[pltpu.VMEM((2, held, latents, width), jnp.bfloat16) for width in widths * 4]
        + [pltpu.VMEM((2, 3 * MAXIMG // 4, latents, width), jnp.bfloat16) for width in widths]
        + [pltpu.VMEM((2 * rows, width), jnp.bfloat16) for width in widths]
        + [
            pltpu.VMEM((2, MAXIMG * latents, max(widths)), jnp.bfloat16),
            pltpu.VMEM((2 * rows, MAXIMG * latents), jnp.float32),
            dma((chunks, 2)),
            dma((chunks, 2)),
            dma((2, chunks, 2)),
            dma((chunks,)),
            dma((chunks,)),
            dma((chunks, 3)),
            dma((chunks, 3)),
            dma((chunks,)),
            dma((chunks,)),
            dma((chunks,)),
        ],
        compiler_params=pltpu.CompilerParams(
            collective_id=0, has_side_effects=True, vmem_limit_bytes=36 * 1024 * 1024
        ),
    )(
        image_slot,
        token_image,
        head_gate,
        token_image.reshape(-1, DH),
        span_first.reshape(-1, DH),
        queries.reshape(rows, all_width),
        image_keys.reshape(held, latents, head_width),
        image_values.reshape(held, latents, head_width),
    )
    return out


def offloaded(head):
    return head % 2 == 0


def split_kernel(
    heads, held, latents, images, few,
    slot_ref, gate_ref, last_ref, first_ref, q_ref, k_ref, v_ref, out_ref, flag_ref, *scratch
):
    own, near, far, q_all, q_end = (scratch[part * heads : (part + 1) * heads] for part in range(5))
    (across, toward, results, win, bias, marks, marks_all, flag_out, flag_in,
     mark_send, mark_recv, mark_sem, flag_sem, own_sem, raw_send, raw_recv, x_send, x_recv,
     y_send, y_recv, q_sem, q_send, q_recv, qe_send, qe_recv, o_send, o_recv) = scratch[5 * heads :]
    rows = q_ref.shape[0]
    tokens = 2 * rows
    half = q_ref.shape[1] // 2
    tiles = tokens // TILE
    per_holder = MAXIMG // 4
    big_slots = 2 * per_holder
    me = lax.axis_index("seq")
    mine = lax.axis_index("tensor")
    other = 1 - mine
    group = lax.axis_index("groups")
    low = me < 2
    end = jnp.where(low, 0, 3)
    mid = jnp.where(low, 1, 2)
    far_mid = 3 - mid
    far_end = 3 - end
    is_end = me == end
    is_mid = me == mid
    peers = [lax.rem(me + d, 4) for d in range(1, 4)]

    barrier = pltpu.get_barrier_semaphore()
    pl.semaphore_signal(barrier, inc=1, device_id={"tensor": other}, device_id_type=MESH)
    pl.semaphore_signal(barrier, inc=1, device_id={"groups": 1 - group}, device_id_type=MESH)
    for peer in peers:
        pl.semaphore_signal(barrier, inc=1, device_id={"seq": peer}, device_id_type=MESH)
    marks_all[me, 0:8] = last_ref[...]
    marks_all[me, 8:16] = first_ref[...]
    pl.semaphore_wait(barrier, 5)

    def remote(src, dst, send, recv, **to):
        return pltpu.make_async_remote_copy(
            src_ref=src, dst_ref=dst, send_sem=send, recv_sem=recv, device_id=to, device_id_type=MESH
        )

    def mark_copy(d, row, to):
        return remote(
            marks_all.at[row], marks_all.at[row], mark_send.at[d], mark_recv.at[row], seq=to
        )

    def cols(c):
        return pl.ds(c * DH, DH)

    def own_copy(c, kv):
        return pltpu.make_async_copy((k_ref, v_ref)[kv].at[:, :, cols(c)], own[c].at[kv], own_sem.at[c, kv])

    def raw_copy(c, kv):
        src = (k_ref, v_ref)[kv].at[:, :, cols(c)]
        return remote(src, near[c].at[kv], raw_send.at[c, kv], raw_recv.at[c, kv], seq=mid)

    def cross_copy(c, part):
        at = pl.ds(0, per_holder) if part == 0 else pl.ds(per_holder, per_holder + few)
        return remote(
            across.at[c, :, at], far[c].at[:, at], x_send.at[c, part], x_recv.at[c, part], seq=far_mid
        )

    def toward_copy(c, part):
        first, second = pl.ds(0, per_holder), pl.ds(per_holder, per_holder)
        src, dst = (
            (toward.at[c // 2, :, first], near[c].at[:, first]),
            (far[c].at[:, first], far[c].at[:, first]),
            (toward.at[c // 2, :, second], far[c].at[:, second]),
        )[part]
        return remote(src, dst, y_send.at[c, part], y_recv.at[c, part], seq=end)

    def q_cols(who, c):
        return pl.ds(pl.multiple_of(who * half + c * DH, DH), DH)

    def q_local(c):
        return pltpu.make_async_copy(
            q_ref.at[:, q_cols(mine, c)], q_all[c].at[pl.ds(mine * rows, rows)], q_sem.at[c]
        )

    def q_remote(c):
        return remote(
            q_ref.at[:, q_cols(other, c)], q_all[c].at[pl.ds(mine * rows, rows)],
            q_send.at[c], q_recv.at[c], tensor=other,
        )

    def q_arrival(c):
        landed = q_all[c].at[pl.ds(other * rows, rows)]
        return remote(landed, landed, q_send.at[c], q_recv.at[c], tensor=other)

    def q_lend(c, part):
        who = (mine, other)[part]
        at = pl.ds(who * rows, rows)
        src = q_ref.at[:, q_cols(mine, c)] if part == 0 else q_all[c].at[at]
        return remote(src, q_end[c].at[at], qe_send.at[c // 2, part], qe_recv.at[c // 2, part], seq=mid)

    def result_copy(c, i):
        at = pl.ds(i * TILE, TILE)
        return remote(
            results.at[c // 2, at], results.at[c // 2, at],
            o_send.at[c // 2, i], o_recv.at[c // 2, i], seq=end,
        )

    def send_pair(p):
        for c in (2 * p, 2 * p + 1):
            for kv in range(2):
                raw_copy(c, kv).start()
        q_lend(2 * p, 0).start()
        q_arrival(2 * p).wait_recv()
        q_lend(2 * p, 1).start()

    for d in range(3):
        mark_copy(d, me, peers[d]).start()
    q_remote(0).start()

    @pl.when(is_end)
    def _():
        for c in (0, 1):
            for kv in range(2):
                raw_copy(c, kv).start()
        q_lend(0, 0).start()

    for c in range(1, heads):
        q_remote(c).start()

    @pl.when(is_end)
    def _():
        q_arrival(0).wait_recv()
        q_lend(0, 1).start()
        for p in range(1, PAIRS_AHEAD):
            send_pair(p)
        for c in range(heads):
            if not offloaded(c):
                for kv in range(2):
                    own_copy(c, kv).start()
                q_local(c).start()

    @pl.when(is_mid)
    def _():
        for c in range(heads):
            for kv in range(2):
                own_copy(c, kv).start()
        for c in range(heads):
            q_local(c).start()

    for d in range(3):
        mark_copy(d, peers[d], peers[d]).wait_recv()
    fetch = pltpu.make_async_copy(marks_all, marks, mark_sem)
    fetch.start()
    fetch.wait()

    def owner_of(row):
        return sum(jnp.where(row >= t * held, 1, 0) for t in range(1, 4))

    slots = [slot_ref[j] for j in range(images)]
    owners = [owner_of(row) for row in slots]

    def base_of(i):
        return jnp.minimum(marks[i, 0, 0], images - MAXIMG)

    def side_plan(left):
        one = jnp.where(left, 0, 2)
        spans = []
        for i in (one, one + 1):
            spans.append((jnp.maximum(base_of(i), marks[i, 8, 0]), marks[i, 7, DH - 1]))
        one_big = spans[0][1] - spans[0][0] >= spans[1][1] - spans[1][0]
        big = jnp.where(one_big, one, one + 1)
        lo = jnp.where(one_big, spans[1][0], spans[0][0])
        hi = jnp.where(one_big, spans[1][1], spans[0][1])
        count = 0
        ids = [0] * few
        for j in range(images):
            away = (owners[j] >= 2) == left
            hit = (j >= lo) & (j <= hi) & away
            ids = [jnp.where(hit & (count == n), j, ids[n]) for n in range(few)]
            count = count + jnp.where(hit, 1, 0)
        return big, ids, count

    here_big, here_ids, here_count = side_plan(low)
    there_big, there_ids, there_count = side_plan(jnp.logical_not(low))
    bad = jnp.where((here_count > few) | (there_count > few), 1, 0)
    flag_out[...] = jnp.zeros(flag_out.shape, jnp.int32) + bad
    flag_copy = remote(flag_out, flag_in, flag_sem.at[0], flag_sem.at[1], groups=1 - group)
    flag_copy.start()

    def held_rows(base, origin):
        found_rows = []
        for k in range(per_holder):
            found = 0
            for t in range(4):
                row = slot_ref[base + 4 * k + t]
                inside = (row >= origin * held) & (row < (origin + 1) * held)
                found = found + jnp.where(inside, row - origin * held, 0)
            found_rows.append(jnp.minimum(found, held - 1))
        return found_rows

    def window(i, at_end):
        base = base_of(i)
        is_big = here_big == i
        places = []
        for w in range(MAXIMG):
            row = slot_ref[base + w]
            owner = owner_of(row)
            local = row - owner * held
            away = (owner >= 2) == low
            slot = 0
            for n in range(few - 1, -1, -1):
                slot = jnp.where(here_ids[n] == base + w, n, slot)
            fewer = jnp.where(at_end, per_holder + lax.rem(slot, per_holder), big_slots + slot)
            place = jnp.where(is_big, jnp.where(owner == far_mid, 0, per_holder) + w // 4, fewer)
            beside = jnp.where(at_end, w // 4, local)
            source = jnp.where(away, 2, jnp.where(owner == me, 0, 1))
            places.append((
                source,
                jnp.where(source == 0, local, 0),
                jnp.where(source == 1, beside, 0),
                jnp.where(source == 2, place, 0),
            ))
        return places

    there_base = base_of(there_big)
    big_mine = held_rows(there_base, me)
    big_near = held_rows(there_base, end)
    end_mine = held_rows(base_of(end), me)
    few_rows = []
    for n in range(few):
        row = slot_ref[there_ids[n]]
        owner = owner_of(row)
        few_rows.append((owner == me, row - owner * held))
    end_far = [
        jnp.where(here_big == end, per_holder + j, big_slots + j % few) for j in range(per_holder)
    ]

    def lend_own(c):
        for k in range(per_holder):
            for kv in range(2):
                across[c, kv, k] = own[c][kv, big_mine[k]]
        cross_copy(c, 0).start()

    def lend_near(c):
        for k in range(per_holder):
            for kv in range(2):
                across[c, kv, per_holder + k] = near[c][kv, big_near[k]]
        for n in range(few):
            is_own, row = few_rows[n]
            for kv in range(2):
                across[c, kv, big_slots + n] = jnp.where(is_own, own[c][kv, row], near[c][kv, row])
        cross_copy(c, 1).start()

    def feed_own(c):
        for k in range(per_holder):
            for kv in range(2):
                toward[c // 2, kv, k] = own[c][kv, end_mine[k]]
        toward_copy(c, 0).start()

    def feed_far(c):
        for j in range(per_holder):
            for kv in range(2):
                toward[c // 2, kv, per_holder + j] = far[c][kv, end_far[j]]
        toward_copy(c, 2).start()

    own_waited = set()

    def need_own(c):
        if c not in own_waited:
            own_waited.add(c)
            for kv in range(2):
                own_copy(c, kv).wait()

    @pl.when(is_mid)
    def _():
        for c in range(max(AHEAD, FEED_AHEAD)):
            need_own(c)
            if c < AHEAD:
                lend_own(c)
            if c < FEED_AHEAD and not offloaded(c):
                feed_own(c)

    def fill_bias(which, i):
        ids = base_of(i) + lax.broadcasted_iota(jnp.int32, (1, MAXIMG * latents), 1) // latents
        for r in range(tokens // DH):
            last = jnp.transpose(jnp.broadcast_to(marks_all[i, r : r + 1, :], (DH, DH)))
            first = jnp.transpose(jnp.broadcast_to(marks_all[i, 8 + r : 9 + r, :], (DH, DH)))
            for at in range(0, MAXIMG * latents, DH):
                part = ids[:, at : at + DH]
                bias[which, r * DH : (r + 1) * DH, at : at + DH] = jnp.where(
                    (part >= first) & (part <= last), 0.0, -1e30
                )

    my_window = window(me, is_end)
    end_window = window(end, False)
    fill_bias(0, me)

    @pl.when(is_mid)
    def _():
        fill_bias(1, end)

    gates = jnp.tanh(gate_ref[...])
    factor = math.log2(math.e) / math.sqrt(DH)

    def fill_window(which, c, places):
        for w in range(MAXIMG):
            source, own_row, near_row, far_row = places[w]
            for kv in range(2):
                image = jnp.where(source == 1, near[c][kv, near_row], own[c][kv, own_row])
                win[which, kv, w * latents : (w + 1) * latents] = jnp.where(
                    source == 2, far[c][kv, far_row], image
                )

    def attend(which, q, c, store):
        gate = gates[:, c : c + 1]

        def tile(i, carry):
            at = pl.ds(pl.multiple_of(i * TILE, TILE), TILE)
            scores = lax.dot_general(
                q[at, :], win[which, 0], (((1,), (1,)), ((), ())), preferred_element_type=jnp.float32
            ) + bias[which, at, :]
            top = jnp.max(scores, axis=1, keepdims=True)
            raised = jnp.exp2((scores - top) * factor)
            total = jnp.sum(raised, axis=1, keepdims=True)
            summed = jnp.dot(
                raised.astype(jnp.bfloat16), win[which, 1], preferred_element_type=jnp.float32
            )
            store(i, at, (summed * (gate / total)).astype(jnp.bfloat16))
            return carry

        lax.fori_loop(0, tiles, tile, 0)

    def own_head(c):
        q_local(c).wait()
        q_arrival(c).wait_recv()
        fill_window(0, c, my_window)

        def store(i, at, value):
            out_ref[at, c * DH : (c + 1) * DH] = value

        attend(0, q_all[c], c, store)

    def end_head(c):
        for part in range(2):
            q_lend(c, part).wait_recv()
        fill_window(1, c, end_window)

        def store(i, at, value):
            results[c // 2, at, :] = value
            result_copy(c, i).start()

        attend(1, q_end[c], c, store)

    def end_wait(c):
        if c // 2 + PAIRS_AHEAD < heads // 2:
            send_pair(c // 2 + PAIRS_AHEAD)
        for kv in range(2):
            own_copy(c, kv).wait()
        for part in range(3):
            toward_copy(c, part).wait_recv()

    for s in range(heads + 2):
        c = s - 1

        @pl.when(is_mid)
        def _():
            if s < heads:
                for kv in range(2):
                    raw_copy(s, kv).wait_recv()
                lend_near(s)
                if s + AHEAD < heads:
                    need_own(s + AHEAD)
                    lend_own(s + AHEAD)
                ahead = s + FEED_AHEAD
                if ahead < heads and not offloaded(ahead):
                    need_own(ahead)
                    feed_own(ahead)
                cross_copy(s, 0).wait_recv()
                if not offloaded(s):
                    toward_copy(s, 1).start()
            if 0 <= c < heads:
                cross_copy(c, 1).wait_recv()
                if offloaded(c):
                    end_head(c)
                else:
                    feed_far(c)
                    own_head(c - 1)

        if 0 <= s - 2 < heads and not offloaded(s - 2):
            pl.when(is_end)(functools.partial(end_wait, s - 2))
            own_head(s - 2)

        if 0 <= c < heads and offloaded(c):
            @pl.when(is_end)
            def _():
                for i in range(tiles):
                    result_copy(c, i).wait_recv()
                out_ref[:, c * DH : (c + 1) * DH] = results[c // 2]

    flag_copy.wait()
    flag_ref[...] = jnp.maximum(flag_out[...], flag_in[...])
    for d in range(3):
        mark_copy(d, me, peers[d]).wait_send()
    for c in range(heads):
        q_remote(c).wait_send()

    @pl.when(is_end)
    def _():
        for c in range(heads):
            for kv in range(2):
                raw_copy(c, kv).wait_send()
            if offloaded(c):
                for part in range(2):
                    q_lend(c, part).wait_send()

    @pl.when(is_mid)
    def _():
        for c in range(heads):
            for part in range(2):
                cross_copy(c, part).wait_send()
            if offloaded(c):
                for i in range(tiles):
                    result_copy(c, i).wait_send()
            else:
                for part in range(3):
                    toward_copy(c, part).wait_send()


def split(queries, image_keys, image_values, head_gate, token_image, span_first, image_slot):
    rows, _, all_width = queries.shape
    held, latents, _, head_width = image_keys.shape
    images = image_slot.shape[0]
    heads = head_width // DH
    tokens = 2 * rows
    tiles = tokens // TILE
    slots = MAXIMG // 2 + FEW
    smem = pl.BlockSpec(memory_space=pltpu.SMEM)
    vmem = pl.BlockSpec(memory_space=pltpu.VMEM)
    hbm = pl.BlockSpec(memory_space=pl.ANY)
    dma = pltpu.SemaphoreType.DMA
    bf16 = jnp.bfloat16
    return pl.pallas_call(
        functools.partial(split_kernel, heads, held, latents, images, FEW),
        out_shape=(pltpu.VMEM((tokens, head_width), bf16), jax.ShapeDtypeStruct((8, DH), jnp.int32)),
        in_specs=[smem, vmem, vmem, vmem, hbm, hbm, hbm],
        out_specs=(vmem, vmem),
        scratch_shapes=[pltpu.VMEM((2, held, latents, DH), bf16)] * (2 * heads)
        + [pltpu.VMEM((2, slots, latents, DH), bf16)] * heads
        + [pltpu.VMEM((tokens, DH), bf16)] * heads
        + [pltpu.VMEM((tokens if offloaded(c) else 16, DH), bf16) for c in range(heads)]
        + [
            pltpu.VMEM((heads, 2, slots, latents, DH), bf16),
            pltpu.VMEM((heads // 2, 2, MAXIMG // 2, latents, DH), bf16),
            pltpu.VMEM((heads // 2, tokens, DH), bf16),
            pltpu.VMEM((2, 2, MAXIMG * latents, DH), bf16),
            pltpu.VMEM((2, tokens, MAXIMG * latents), jnp.float32),
            pltpu.SMEM((4, 16, DH), jnp.int32),
            pltpu.VMEM((4, 16, DH), jnp.int32),
            pltpu.VMEM((8, DH), jnp.int32),
            pltpu.VMEM((8, DH), jnp.int32),
            dma((3,)),
            dma((4,)),
            dma,
            dma((2,)),
            dma((heads, 2)),
            dma((heads, 2)),
            dma((heads, 2)),
            dma((heads, 2)),
            dma((heads, 2)),
            dma((heads, 3)),
            dma((heads, 3)),
            dma((heads,)),
            dma((heads,)),
            dma((heads,)),
            dma((heads // 2, 2)),
            dma((heads // 2, 2)),
            dma((heads // 2, tiles)),
            dma((heads // 2, tiles)),
        ],
        compiler_params=pltpu.CompilerParams(
            collective_id=1, has_side_effects=True, vmem_limit_bytes=40 * 1024 * 1024
        ),
    )(
        image_slot,
        head_gate,
        token_image.reshape(-1, DH),
        span_first.reshape(-1, DH),
        queries.reshape(rows, all_width),
        image_keys.reshape(held, latents, head_width),
        image_values.reshape(held, latents, head_width),
    )


def attended(*args):
    result, flag = split(*args)
    bad = flag[0, 0]
    kept = jnp.where(args[4][0] < 0, jnp.bfloat16(0), result)
    result = lax.while_loop(
        lambda c: c[0] > 0, lambda c: (0, jnp.where(c[0] > 0, fused(*args), c[1])), (bad, kept)
    )[1]
    return result.reshape(result.shape[0], 1, result.shape[1])


def lookup(lookup_table, at_index):
    count = lookup_table.shape[0]
    hits = jnp.arange(count, dtype=jnp.int32) == at_index[..., None]
    return jnp.sum(jnp.where(hits, lookup_table, 0), axis=-1)


def per_device(queries, image_keys, image_values, head_gate, token_image, span_first, image_slot):
    tensor_count = lax.axis_size("tensor")
    row_count = queries.shape[0]
    half_width = queries.shape[2]
    split_rows = queries.reshape(row_count, tensor_count, half_width // tensor_count)
    head_rows = lax.all_to_all(split_rows, "tensor", split_axis=1, concat_axis=0, tiled=True)
    token_count = head_rows.shape[0]
    head_width = head_rows.shape[2]
    head_count = head_width // DH
    held_count = image_keys.shape[0]
    latents = image_keys.shape[1]
    images = image_slot.shape[0]
    packed = jnp.concatenate([image_keys[:, :, 0, :], image_values[:, :, 0, :]], axis=2)
    packed = packed.reshape(held_count, latents * 2 * head_width)
    window_start = jnp.minimum(token_image[0], images - MAXIMG)
    window_ids = window_start + jnp.arange(MAXIMG, dtype=jnp.int32)
    in_window = window_ids < images
    safe_ids = jnp.minimum(window_ids, images - 1)
    window_slot = lookup(image_slot, safe_ids)
    fragment = lax.all_gather(packed, "seq", axis=0, tiled=True)
    piece_rows = jnp.arange(fragment.shape[0], dtype=jnp.int32)
    select = ((window_slot[:, None] == piece_rows[None, :]) & in_window[:, None]).astype(
        jnp.bfloat16
    )
    window = jnp.dot(select, fragment, preferred_element_type=jnp.float32).astype(jnp.bfloat16)
    window = window.reshape(MAXIMG * latents, 2 * head_width)
    keys_win = window[:, :head_width]
    values_win = window[:, head_width:]
    visible = (window_ids[None, :] >= span_first[:, None]) & (
        window_ids[None, :] <= token_image[:, None]
    )
    key_mask = jnp.repeat(visible, latents, axis=1)
    score_scale = 1.0 / math.sqrt(DH)
    gate_values = jnp.tanh(head_gate.reshape(-1))
    results = []
    for head_index in range(head_count):
        low_col = head_index * DH
        head_query = head_rows[:, 0, low_col : low_col + DH]
        scores = (
            lax.dot_general(
                head_query,
                keys_win[:, low_col : low_col + DH],
                (((1,), (1,)), ((), ())),
                preferred_element_type=jnp.float32,
            )
            * score_scale
        )
        row_top = jnp.max(jnp.where(key_mask, scores, -1e30), axis=1, keepdims=True)
        raised = jnp.exp(jnp.where(key_mask, scores - row_top, -1e30))
        row_total = jnp.sum(raised, axis=1, keepdims=True)
        weights = raised.astype(jnp.bfloat16)
        summed = jnp.dot(
            weights, values_win[:, low_col : low_col + DH], preferred_element_type=jnp.float32
        )
        results.append(summed / row_total * gate_values[head_index])
    attended = jnp.concatenate(results, axis=1).astype(jnp.bfloat16)
    return attended.reshape(token_count, 1, head_width)


def solution(mesh):
    placed = (
        P(("groups", "seq", "tensor"), "sub", None),
        P(("groups", "seq"), None, "sub", "tensor"),
        P(("groups", "seq"), None, "sub", "tensor"),
        P("sub", "tensor"),
        P(("groups", "seq")),
        P(("groups", "seq")),
        P("groups"),
    )
    fits = mesh.shape["seq"] == 4 and mesh.shape["tensor"] == 2
    return jax.shard_map(
        attended if fits else per_device,
        mesh=mesh,
        in_specs=placed,
        out_specs=P(("groups", "seq"), "sub", "tensor"),
        check_vma=False,
    )
```

```python
import functools
import math

import jax
import jax.numpy as jnp
from jax import lax
from jax.experimental import pallas as pl
from jax.experimental.pallas import tpu as pltpu
from jax.sharding import PartitionSpec as P

DH = 128
MAXIMG = 16
TILE = 512
LEAD = 3
AHEAD = 2
FEED_AHEAD = 8
PAIRS_AHEAD = 3
FEW = 2
MESH = pl.DeviceIdType.MESH


def fused_kernel(
    plan, held, latents, images,
    slot_ref, tok_ref, gate_ref, last_ref, first_ref, q_ref, k_ref, v_ref, out_ref, *scratch
):
    chunks = len(plan)
    starts = [sum(plan[:c]) * DH for c in range(chunks)]
    widths = [heads * DH for heads in plan]
    own, near, far, farthest, sel, q_all = (
        scratch[part * chunks : (part + 1) * chunks] for part in range(6)
    )
    (win, bias, own_sem, raw_send, raw_recv, rel_send, rel_recv,
     sel_send, sel_recv, q_sem, q_send, q_recv) = scratch[6 * chunks :]
    rows = q_ref.shape[0]
    half = q_ref.shape[1] // 2
    per_holder = MAXIMG // 4
    me = lax.axis_index("seq")
    mine = lax.axis_index("tensor")
    other = 1 - mine
    low = me < 2
    end = jnp.where(low, 0, 3)
    mid = jnp.where(low, 1, 2)
    far_mid = 3 - mid
    far_end = 3 - end
    is_end = me == end
    is_mid = me == mid
    peer = jnp.where(is_end, mid, far_mid)

    barrier = pltpu.get_barrier_semaphore()
    pl.semaphore_signal(barrier, inc=1, device_id={"tensor": other}, device_id_type=MESH)

    @pl.when(is_end)
    def _():
        pl.semaphore_signal(barrier, inc=1, device_id={"seq": mid}, device_id_type=MESH)
        pl.semaphore_wait(barrier, 2)

    @pl.when(is_mid)
    def _():
        pl.semaphore_signal(barrier, inc=1, device_id={"seq": end}, device_id_type=MESH)
        pl.semaphore_signal(barrier, inc=1, device_id={"seq": far_mid}, device_id_type=MESH)
        pl.semaphore_wait(barrier, 3)

    def cols(c):
        return pl.ds(starts[c], widths[c])

    def own_copy(c, kv):
        src = (k_ref, v_ref)[kv]
        return pltpu.make_async_copy(src.at[:, :, cols(c)], own[c].at[kv], own_sem.at[c, kv])

    def raw_copy(c, kv, frm, to):
        src = (k_ref, v_ref)[kv]
        which = 0 if frm is end else 1
        return pltpu.make_async_remote_copy(
            src_ref=src.at[:, :, cols(c)],
            dst_ref=(near, far)[which][c].at[kv],
            send_sem=raw_send.at[c, kv],
            recv_sem=raw_recv.at[which, c, kv],
            device_id={"seq": to},
            device_id_type=MESH,
        )

    def relay_copy(c):
        return pltpu.make_async_remote_copy(
            src_ref=near[c], dst_ref=farthest[c],
            send_sem=rel_send.at[c], recv_sem=rel_recv.at[c],
            device_id={"seq": far_mid}, device_id_type=MESH,
        )

    origins = (mid, far_mid, far_end)

    def sel_copy(c, n):
        return pltpu.make_async_remote_copy(
            src_ref=sel[c].at[:, pl.ds(n * per_holder, per_holder)],
            dst_ref=(near, far, farthest)[n][c].at[:, pl.ds(0, per_holder)],
            send_sem=sel_send.at[c, n],
            recv_sem=sel_recv.at[c, n],
            device_id={"seq": end},
            device_id_type=MESH,
        )

    def q_local(c):
        return pltpu.make_async_copy(
            q_ref.at[:, pl.ds(pl.multiple_of(mine * half + starts[c], DH), widths[c])],
            q_all[c].at[pl.ds(mine * rows, rows)],
            q_sem.at[c],
        )

    def q_remote(c):
        return pltpu.make_async_remote_copy(
            src_ref=q_ref.at[:, pl.ds(pl.multiple_of(other * half + starts[c], DH), widths[c])],
            dst_ref=q_all[c].at[pl.ds(mine * rows, rows)],
            send_sem=q_send.at[c],
            recv_sem=q_recv.at[c],
            device_id={"tensor": other},
            device_id_type=MESH,
        )

    def q_arrival(c):
        return pltpu.make_async_remote_copy(
            src_ref=q_all[c].at[pl.ds(other * rows, rows)],
            dst_ref=q_all[c].at[pl.ds(other * rows, rows)],
            send_sem=q_send.at[c],
            recv_sem=q_recv.at[c],
            device_id={"tensor": other},
            device_id_type=MESH,
        )

    @pl.when(is_end)
    def _():
        for c in range(chunks):
            for kv in range(2):
                raw_copy(c, kv, end, mid).start()

    @pl.when(is_mid)
    def _():
        for c in range(min(2, chunks)):
            for kv in range(2):
                raw_copy(c, kv, mid, far_mid).start()

    for c in range(chunks):
        q_remote(c).start()
    for c in range(chunks):
        for kv in range(2):
            own_copy(c, kv).start()
        q_local(c).start()

    base = jnp.where(
        me == 0, 0, jnp.where(me == 3, images - MAXIMG, jnp.minimum(tok_ref[0], images - MAXIMG))
    )
    neighbour = jnp.where(is_end, mid, end)
    window_rows = []
    for w in range(MAXIMG):
        row = slot_ref[base + w]
        owner = sum(jnp.where(row >= t * held, 1, 0) for t in range(1, 4))
        local = jnp.where(is_end & (owner != me), w // 4, row - owner * held)
        window_rows.append((owner, local))
    end_base = jnp.where(low, 0, images - MAXIMG)
    sel_rows = []
    for origin in origins:
        for k in range(per_holder):
            found = 0
            for t in range(4):
                row = slot_ref[end_base + 4 * k + t]
                inside = (row >= origin * held) & (row < (origin + 1) * held)
                found = found + jnp.where(inside, row - origin * held, 0)
            sel_rows.append(found)

    def send_selected(c, n):
        source = (own, far, farthest)[n][c]
        for at in range(n * per_holder, (n + 1) * per_holder):
            for kv in range(2):
                sel[c][kv, at] = source[kv, sel_rows[at]]
        sel_copy(c, n).start()

    def send_own(c):
        for kv in range(2):
            own_copy(c, kv).wait()
        send_selected(c, 0)

    def pick(c, kv, owner, local):
        image = own[c][kv, local]
        for part, holder in ((near, neighbour), (far, far_mid), (farthest, far_end)):
            image = jnp.where(owner == holder, part[c][kv, local], image)
        return image

    @pl.when(is_mid)
    def _():
        for c in range(LEAD):
            send_own(c)

    tokens = 2 * rows
    ids = base + lax.broadcasted_iota(jnp.int32, (1, MAXIMG * latents), 1) // latents
    for r in range(tokens // DH):
        last = jnp.transpose(jnp.broadcast_to(last_ref[r : r + 1, :], (DH, DH)))
        first = jnp.transpose(jnp.broadcast_to(first_ref[r : r + 1, :], (DH, DH)))
        for at in range(0, MAXIMG * latents, DH):
            part = ids[:, at : at + DH]
            bias[r * DH : (r + 1) * DH, at : at + DH] = jnp.where(
                (part >= first) & (part <= last), 0.0, -1e30
            )
    gates = jnp.tanh(gate_ref[...])
    factor = math.log2(math.e) / math.sqrt(DH)

    for s in range(chunks + 2):
        if s < chunks:
            @pl.when(is_mid)
            def _():
                for kv in range(2):
                    raw_copy(s, kv, end, mid).wait_recv()
                relay_copy(s).start()
                if s + 2 < chunks:
                    for kv in range(2):
                        raw_copy(s + 2, kv, mid, far_mid).start()
        if 0 <= s - 1 < chunks:
            c = s - 1

            @pl.when(is_mid)
            def _():
                for kv in range(2):
                    raw_copy(c, kv, far_mid, mid).wait_recv()
                send_selected(c, 1)
                relay_copy(c).wait_recv()
                send_selected(c, 2)
                if c + LEAD < chunks:
                    send_own(c + LEAD)

        if 0 <= s - 2 < chunks:
            c = s - 2

            @pl.when(is_end)
            def _():
                for kv in range(2):
                    own_copy(c, kv).wait()
                for n in range(3):
                    sel_copy(c, n).wait_recv()

            q_local(c).wait()
            q_arrival(c).wait_recv()
            for w in range(MAXIMG):
                for kv in range(2):
                    win[kv, w * latents : (w + 1) * latents, : widths[c]] = pick(c, kv, *window_rows[w])

            def attend(i, carry):
                at = pl.ds(i * TILE, TILE)
                for h in range(plan[c]):
                    lane = slice(h * DH, (h + 1) * DH)
                    scores = lax.dot_general(
                        q_all[c][at, lane], win[0, :, lane], (((1,), (1,)), ((), ())),
                        preferred_element_type=jnp.float32,
                    ) + bias[at, :]
                    top = jnp.max(scores, axis=1, keepdims=True)
                    raised = jnp.exp2((scores - top) * factor)
                    total = jnp.sum(raised, axis=1, keepdims=True)
                    summed = jnp.dot(
                        raised.astype(jnp.bfloat16), win[1, :, lane],
                        preferred_element_type=jnp.float32,
                    )
                    at_col = starts[c] + h * DH
                    gate = gates[:, at_col // DH : at_col // DH + 1]
                    out_ref[at, at_col : at_col + DH] = (summed * (gate / total)).astype(
                        jnp.bfloat16
                    )
                return carry

            lax.fori_loop(0, tokens // TILE, attend, 0)

    for c in range(chunks):
        q_remote(c).wait_send()

    @pl.when(is_end)
    def _():
        for c in range(chunks):
            for kv in range(2):
                raw_copy(c, kv, end, mid).wait_send()

    @pl.when(is_mid)
    def _():
        for c in range(chunks):
            for kv in range(2):
                raw_copy(c, kv, mid, far_mid).wait_send()
            relay_copy(c).wait_send()
            for n in range(3):
                sel_copy(c, n).wait_send()


def fused(queries, image_keys, image_values, head_gate, token_image, span_first, image_slot):
    rows, _, all_width = queries.shape
    held, latents, _, head_width = image_keys.shape
    images = image_slot.shape[0]
    heads = head_width // DH
    plan = (1, 1) + (2,) * ((heads - 4) // 2) + (1, 1)
    chunks = len(plan)
    widths = [count * DH for count in plan]
    smem = pl.BlockSpec(memory_space=pltpu.SMEM)
    vmem = pl.BlockSpec(memory_space=pltpu.VMEM)
    hbm = pl.BlockSpec(memory_space=pl.ANY)
    dma = pltpu.SemaphoreType.DMA
    out = pl.pallas_call(
        functools.partial(fused_kernel, plan, held, latents, images),
        out_shape=jax.ShapeDtypeStruct((2 * rows, head_width), jnp.bfloat16),
        in_specs=[smem, smem, vmem, vmem, vmem, hbm, hbm, hbm],
        out_specs=vmem,
        scratch_shapes=[pltpu.VMEM((2, held, latents, width), jnp.bfloat16) for width in widths * 4]
        + [pltpu.VMEM((2, 3 * MAXIMG // 4, latents, width), jnp.bfloat16) for width in widths]
        + [pltpu.VMEM((2 * rows, width), jnp.bfloat16) for width in widths]
        + [
            pltpu.VMEM((2, MAXIMG * latents, max(widths)), jnp.bfloat16),
            pltpu.VMEM((2 * rows, MAXIMG * latents), jnp.float32),
            dma((chunks, 2)),
            dma((chunks, 2)),
            dma((2, chunks, 2)),
            dma((chunks,)),
            dma((chunks,)),
            dma((chunks, 3)),
            dma((chunks, 3)),
            dma((chunks,)),
            dma((chunks,)),
            dma((chunks,)),
        ],
        compiler_params=pltpu.CompilerParams(
            collective_id=0, has_side_effects=True, vmem_limit_bytes=36 * 1024 * 1024
        ),
    )(
        image_slot,
        token_image,
        head_gate,
        token_image.reshape(-1, DH),
        span_first.reshape(-1, DH),
        queries.reshape(rows, all_width),
        image_keys.reshape(held, latents, head_width),
        image_values.reshape(held, latents, head_width),
    )
    return out


def offloaded(head, heads):
    return head % 2 == 0 and head < heads - 2


def split_kernel(
    heads, held, latents, images, few,
    slot_ref, gate_ref, last_ref, first_ref, q_ref, k_ref, v_ref, out_ref, flag_ref, *scratch
):
    own, near, far, q_all, q_end = (scratch[part * heads : (part + 1) * heads] for part in range(5))
    (across, toward, results, win, bias, marks, marks_all, flag_out, flag_in,
     mark_send, mark_recv, mark_sem, flag_sem, own_sem, raw_send, raw_recv, x_send, x_recv,
     y_send, y_recv, q_sem, q_send, q_recv, qe_send, qe_recv, o_send, o_recv) = scratch[5 * heads :]
    rows = q_ref.shape[0]
    tokens = 2 * rows
    half = q_ref.shape[1] // 2
    tiles = tokens // TILE
    per_holder = MAXIMG // 4
    big_slots = 2 * per_holder
    me = lax.axis_index("seq")
    mine = lax.axis_index("tensor")
    other = 1 - mine
    group = lax.axis_index("groups")
    low = me < 2
    end = jnp.where(low, 0, 3)
    mid = jnp.where(low, 1, 2)
    far_mid = 3 - mid
    far_end = 3 - end
    is_end = me == end
    is_mid = me == mid
    peers = [lax.rem(me + d, 4) for d in range(1, 4)]

    barrier = pltpu.get_barrier_semaphore()
    pl.semaphore_signal(barrier, inc=1, device_id={"tensor": other}, device_id_type=MESH)
    pl.semaphore_signal(barrier, inc=1, device_id={"groups": 1 - group}, device_id_type=MESH)
    for peer in peers:
        pl.semaphore_signal(barrier, inc=1, device_id={"seq": peer}, device_id_type=MESH)
    marks_all[me, 0:8] = last_ref[...]
    marks_all[me, 8:16] = first_ref[...]
    pl.semaphore_wait(barrier, 5)

    def remote(src, dst, send, recv, **to):
        return pltpu.make_async_remote_copy(
            src_ref=src, dst_ref=dst, send_sem=send, recv_sem=recv, device_id=to, device_id_type=MESH
        )

    def mark_copy(d, row, to):
        return remote(
            marks_all.at[row], marks_all.at[row], mark_send.at[d], mark_recv.at[row], seq=to
        )

    def cols(c):
        return pl.ds(c * DH, DH)

    def own_copy(c, kv):
        return pltpu.make_async_copy((k_ref, v_ref)[kv].at[:, :, cols(c)], own[c].at[kv], own_sem.at[c, kv])

    def raw_copy(c, kv):
        src = (k_ref, v_ref)[kv].at[:, :, cols(c)]
        return remote(src, near[c].at[kv], raw_send.at[c, kv], raw_recv.at[c, kv], seq=mid)

    def cross_copy(c, part):
        at = pl.ds(0, per_holder) if part == 0 else pl.ds(per_holder, per_holder + few)
        return remote(
            across.at[c, :, at], far[c].at[:, at], x_send.at[c, part], x_recv.at[c, part], seq=far_mid
        )

    def toward_copy(c, part):
        first, second = pl.ds(0, per_holder), pl.ds(per_holder, per_holder)
        src, dst = (
            (toward.at[c, :, first], near[c].at[:, first]),
            (far[c].at[:, first], far[c].at[:, first]),
            (toward.at[c, :, second], far[c].at[:, second]),
        )[part]
        return remote(src, dst, y_send.at[c, part], y_recv.at[c, part], seq=end)

    def q_cols(who, c):
        return pl.ds(pl.multiple_of(who * half + c * DH, DH), DH)

    def q_local(c):
        return pltpu.make_async_copy(
            q_ref.at[:, q_cols(mine, c)], q_all[c].at[pl.ds(mine * rows, rows)], q_sem.at[c]
        )

    def q_remote(c):
        return remote(
            q_ref.at[:, q_cols(other, c)], q_all[c].at[pl.ds(mine * rows, rows)],
            q_send.at[c], q_recv.at[c], tensor=other,
        )

    def q_arrival(c):
        landed = q_all[c].at[pl.ds(other * rows, rows)]
        return remote(landed, landed, q_send.at[c], q_recv.at[c], tensor=other)

    def q_lend(c, part):
        who = (mine, other)[part]
        at = pl.ds(who * rows, rows)
        src = q_ref.at[:, q_cols(mine, c)] if part == 0 else q_all[c].at[at]
        return remote(src, q_end[c].at[at], qe_send.at[c // 2, part], qe_recv.at[c // 2, part], seq=mid)

    def result_copy(c, i):
        at = pl.ds(i * TILE, TILE)
        return remote(
            results.at[c // 2, at], results.at[c // 2, at],
            o_send.at[c // 2, i], o_recv.at[c // 2, i], seq=end,
        )

    def send_pair(p):
        for c in (2 * p, 2 * p + 1):
            for kv in range(2):
                raw_copy(c, kv).start()
        if offloaded(2 * p, heads):
            q_lend(2 * p, 0).start()
            q_arrival(2 * p).wait_recv()
            q_lend(2 * p, 1).start()

    for d in range(3):
        mark_copy(d, me, peers[d]).start()
    q_remote(0).start()

    @pl.when(is_end)
    def _():
        for c in (0, 1):
            for kv in range(2):
                raw_copy(c, kv).start()
        q_lend(0, 0).start()

    for c in range(1, heads):
        q_remote(c).start()

    @pl.when(is_end)
    def _():
        q_arrival(0).wait_recv()
        q_lend(0, 1).start()
        for p in range(1, PAIRS_AHEAD):
            send_pair(p)
        for c in range(heads):
            if not offloaded(c, heads):
                for kv in range(2):
                    own_copy(c, kv).start()
                q_local(c).start()

    @pl.when(is_mid)
    def _():
        for c in range(heads):
            for kv in range(2):
                own_copy(c, kv).start()
        for c in range(heads):
            q_local(c).start()

    for d in range(3):
        mark_copy(d, peers[d], peers[d]).wait_recv()
    fetch = pltpu.make_async_copy(marks_all, marks, mark_sem)
    fetch.start()
    fetch.wait()

    def owner_of(row):
        return sum(jnp.where(row >= t * held, 1, 0) for t in range(1, 4))

    slots = [slot_ref[j] for j in range(images)]
    owners = [owner_of(row) for row in slots]

    def base_of(i):
        return jnp.minimum(marks[i, 0, 0], images - MAXIMG)

    def side_plan(left):
        one = jnp.where(left, 0, 2)
        spans = []
        for i in (one, one + 1):
            spans.append((jnp.maximum(base_of(i), marks[i, 8, 0]), marks[i, 7, DH - 1]))
        one_big = spans[0][1] - spans[0][0] >= spans[1][1] - spans[1][0]
        big = jnp.where(one_big, one, one + 1)
        lo = jnp.where(one_big, spans[1][0], spans[0][0])
        hi = jnp.where(one_big, spans[1][1], spans[0][1])
        count = 0
        ids = [0] * few
        for j in range(images):
            away = (owners[j] >= 2) == left
            hit = (j >= lo) & (j <= hi) & away
            ids = [jnp.where(hit & (count == n), j, ids[n]) for n in range(few)]
            count = count + jnp.where(hit, 1, 0)
        return big, ids, count

    here_big, here_ids, here_count = side_plan(low)
    there_big, there_ids, there_count = side_plan(jnp.logical_not(low))
    bad = jnp.where((here_count > few) | (there_count > few), 1, 0)
    flag_out[...] = jnp.zeros(flag_out.shape, jnp.int32) + bad
    flag_copy = remote(flag_out, flag_in, flag_sem.at[0], flag_sem.at[1], groups=1 - group)
    flag_copy.start()

    def held_rows(base, origin):
        found_rows = []
        for k in range(per_holder):
            found = 0
            for t in range(4):
                row = slot_ref[base + 4 * k + t]
                inside = (row >= origin * held) & (row < (origin + 1) * held)
                found = found + jnp.where(inside, row - origin * held, 0)
            found_rows.append(jnp.minimum(found, held - 1))
        return found_rows

    def window(i, at_end):
        base = base_of(i)
        is_big = here_big == i
        places = []
        for w in range(MAXIMG):
            row = slot_ref[base + w]
            owner = owner_of(row)
            local = row - owner * held
            away = (owner >= 2) == low
            slot = 0
            for n in range(few - 1, -1, -1):
                slot = jnp.where(here_ids[n] == base + w, n, slot)
            fewer = jnp.where(at_end, per_holder + lax.rem(slot, per_holder), big_slots + slot)
            place = jnp.where(is_big, jnp.where(owner == far_mid, 0, per_holder) + w // 4, fewer)
            beside = jnp.where(at_end, w // 4, local)
            source = jnp.where(away, 2, jnp.where(owner == me, 0, 1))
            places.append((
                source,
                jnp.where(source == 0, local, 0),
                jnp.where(source == 1, beside, 0),
                jnp.where(source == 2, place, 0),
            ))
        return places

    there_base = base_of(there_big)
    big_mine = held_rows(there_base, me)
    big_near = held_rows(there_base, end)
    end_mine = held_rows(base_of(end), me)
    few_rows = []
    for n in range(few):
        row = slot_ref[there_ids[n]]
        owner = owner_of(row)
        few_rows.append((owner == me, row - owner * held))
    end_far = [
        jnp.where(here_big == end, per_holder + j, big_slots + j % few) for j in range(per_holder)
    ]

    def lend_own(c):
        for k in range(per_holder):
            for kv in range(2):
                across[c, kv, k] = own[c][kv, big_mine[k]]
        cross_copy(c, 0).start()

    def lend_near(c):
        for k in range(per_holder):
            for kv in range(2):
                across[c, kv, per_holder + k] = near[c][kv, big_near[k]]
        for n in range(few):
            is_own, row = few_rows[n]
            for kv in range(2):
                across[c, kv, big_slots + n] = jnp.where(is_own, own[c][kv, row], near[c][kv, row])
        cross_copy(c, 1).start()

    def feed_own(c):
        for k in range(per_holder):
            for kv in range(2):
                toward[c, kv, k] = own[c][kv, end_mine[k]]
        toward_copy(c, 0).start()

    def feed_far(c):
        for j in range(per_holder):
            for kv in range(2):
                toward[c, kv, per_holder + j] = far[c][kv, end_far[j]]
        toward_copy(c, 2).start()

    own_waited = set()

    def need_own(c):
        if c not in own_waited:
            own_waited.add(c)
            for kv in range(2):
                own_copy(c, kv).wait()

    @pl.when(is_mid)
    def _():
        for c in range(max(AHEAD, FEED_AHEAD)):
            need_own(c)
            if c < AHEAD:
                lend_own(c)
            if c < FEED_AHEAD and not offloaded(c, heads):
                feed_own(c)

    def fill_bias(which, i):
        ids = base_of(i) + lax.broadcasted_iota(jnp.int32, (1, MAXIMG * latents), 1) // latents
        for r in range(tokens // DH):
            last = jnp.transpose(jnp.broadcast_to(marks_all[i, r : r + 1, :], (DH, DH)))
            first = jnp.transpose(jnp.broadcast_to(marks_all[i, 8 + r : 9 + r, :], (DH, DH)))
            for at in range(0, MAXIMG * latents, DH):
                part = ids[:, at : at + DH]
                bias[which, r * DH : (r + 1) * DH, at : at + DH] = jnp.where(
                    (part >= first) & (part <= last), 0.0, -1e30
                )

    my_window = window(me, is_end)
    end_window = window(end, False)
    fill_bias(0, me)

    @pl.when(is_mid)
    def _():
        fill_bias(1, end)

    gates = jnp.tanh(gate_ref[...])
    factor = math.log2(math.e) / math.sqrt(DH)

    def fill_window(which, c, places):
        for w in range(MAXIMG):
            source, own_row, near_row, far_row = places[w]
            for kv in range(2):
                image = jnp.where(source == 1, near[c][kv, near_row], own[c][kv, own_row])
                win[which, kv, w * latents : (w + 1) * latents] = jnp.where(
                    source == 2, far[c][kv, far_row], image
                )

    def attend(which, q, c, store):
        gate = gates[:, c : c + 1]

        def tile(i, carry):
            at = pl.ds(pl.multiple_of(i * TILE, TILE), TILE)
            scores = lax.dot_general(
                q[at, :], win[which, 0], (((1,), (1,)), ((), ())), preferred_element_type=jnp.float32
            ) + bias[which, at, :]
            top = jnp.max(scores, axis=1, keepdims=True)
            raised = jnp.exp2((scores - top) * factor)
            total = jnp.sum(raised, axis=1, keepdims=True)
            summed = jnp.dot(
                raised.astype(jnp.bfloat16), win[which, 1], preferred_element_type=jnp.float32
            )
            store(i, at, (summed * (gate / total)).astype(jnp.bfloat16))
            return carry

        lax.fori_loop(0, tiles, tile, 0)

    def own_head(c):
        q_local(c).wait()
        q_arrival(c).wait_recv()
        fill_window(0, c, my_window)

        def store(i, at, value):
            out_ref[at, c * DH : (c + 1) * DH] = value

        attend(0, q_all[c], c, store)

    def end_head(c):
        for part in range(2):
            q_lend(c, part).wait_recv()
        fill_window(1, c, end_window)

        def store(i, at, value):
            results[c // 2, at, :] = value
            result_copy(c, i).start()

        attend(1, q_end[c], c, store)

    def end_wait(c):
        if c % 2 == 1 and c // 2 + PAIRS_AHEAD < heads // 2:
            send_pair(c // 2 + PAIRS_AHEAD)
        for kv in range(2):
            own_copy(c, kv).wait()
        for part in range(3):
            toward_copy(c, part).wait_recv()

    for s in range(heads + 2):
        c = s - 1

        @pl.when(is_mid)
        def _():
            if s < heads:
                for kv in range(2):
                    raw_copy(s, kv).wait_recv()
                lend_near(s)
                if s + AHEAD < heads:
                    need_own(s + AHEAD)
                    lend_own(s + AHEAD)
                ahead = s + FEED_AHEAD
                if ahead < heads and not offloaded(ahead, heads):
                    need_own(ahead)
                    feed_own(ahead)
                cross_copy(s, 0).wait_recv()
                if not offloaded(s, heads):
                    toward_copy(s, 1).start()
            if 0 <= c < heads:
                cross_copy(c, 1).wait_recv()
                if offloaded(c, heads):
                    end_head(c)
                else:
                    feed_far(c)
                    if offloaded(c - 1, heads):
                        own_head(c - 1)

        if 0 <= s - 2 < heads and not offloaded(s - 2, heads):
            pl.when(is_end)(functools.partial(end_wait, s - 2))
            own_head(s - 2)

        if 0 <= c < heads and offloaded(c, heads):
            @pl.when(is_end)
            def _():
                for i in range(tiles):
                    result_copy(c, i).wait_recv()
                out_ref[:, c * DH : (c + 1) * DH] = results[c // 2]

    flag_copy.wait()
    flag_ref[...] = jnp.maximum(flag_out[...], flag_in[...])
    for d in range(3):
        mark_copy(d, me, peers[d]).wait_send()
    for c in range(heads):
        q_remote(c).wait_send()

    @pl.when(is_end)
    def _():
        for c in range(heads):
            for kv in range(2):
                raw_copy(c, kv).wait_send()
            if offloaded(c, heads):
                for part in range(2):
                    q_lend(c, part).wait_send()

    @pl.when(is_mid)
    def _():
        for c in range(heads):
            for part in range(2):
                cross_copy(c, part).wait_send()
            if offloaded(c, heads):
                for i in range(tiles):
                    result_copy(c, i).wait_send()
            else:
                for part in range(3):
                    toward_copy(c, part).wait_send()


def split(queries, image_keys, image_values, head_gate, token_image, span_first, image_slot):
    rows, _, all_width = queries.shape
    held, latents, _, head_width = image_keys.shape
    images = image_slot.shape[0]
    heads = head_width // DH
    tokens = 2 * rows
    tiles = tokens // TILE
    slots = MAXIMG // 2 + FEW
    smem = pl.BlockSpec(memory_space=pltpu.SMEM)
    vmem = pl.BlockSpec(memory_space=pltpu.VMEM)
    hbm = pl.BlockSpec(memory_space=pl.ANY)
    dma = pltpu.SemaphoreType.DMA
    bf16 = jnp.bfloat16
    return pl.pallas_call(
        functools.partial(split_kernel, heads, held, latents, images, FEW),
        out_shape=(pltpu.VMEM((tokens, head_width), bf16), jax.ShapeDtypeStruct((8, DH), jnp.int32)),
        in_specs=[smem, vmem, vmem, vmem, hbm, hbm, hbm],
        out_specs=(vmem, vmem),
        scratch_shapes=[pltpu.VMEM((2, held, latents, DH), bf16)] * (2 * heads)
        + [pltpu.VMEM((2, slots, latents, DH), bf16)] * heads
        + [pltpu.VMEM((tokens, DH), bf16)] * heads
        + [pltpu.VMEM((tokens if offloaded(c, heads) else 16, DH), bf16) for c in range(heads)]
        + [
            pltpu.VMEM((heads, 2, slots, latents, DH), bf16),
            pltpu.VMEM((heads, 2, MAXIMG // 2, latents, DH), bf16),
            pltpu.VMEM((heads // 2, tokens, DH), bf16),
            pltpu.VMEM((2, 2, MAXIMG * latents, DH), bf16),
            pltpu.VMEM((2, tokens, MAXIMG * latents), jnp.float32),
            pltpu.SMEM((4, 16, DH), jnp.int32),
            pltpu.VMEM((4, 16, DH), jnp.int32),
            pltpu.VMEM((8, DH), jnp.int32),
            pltpu.VMEM((8, DH), jnp.int32),
            dma((3,)),
            dma((4,)),
            dma,
            dma((2,)),
            dma((heads, 2)),
            dma((heads, 2)),
            dma((heads, 2)),
            dma((heads, 2)),
            dma((heads, 2)),
            dma((heads, 3)),
            dma((heads, 3)),
            dma((heads,)),
            dma((heads,)),
            dma((heads,)),
            dma((heads // 2, 2)),
            dma((heads // 2, 2)),
            dma((heads // 2, tiles)),
            dma((heads // 2, tiles)),
        ],
        compiler_params=pltpu.CompilerParams(
            collective_id=1, has_side_effects=True, vmem_limit_bytes=43 * 1024 * 1024
        ),
    )(
        image_slot,
        head_gate,
        token_image.reshape(-1, DH),
        span_first.reshape(-1, DH),
        queries.reshape(rows, all_width),
        image_keys.reshape(held, latents, head_width),
        image_values.reshape(held, latents, head_width),
    )


def attended(*args):
    result, flag = split(*args)
    bad = flag[0, 0]
    kept = jnp.where(args[4][0] < 0, jnp.bfloat16(0), result)
    result = lax.while_loop(
        lambda c: c[0] > 0, lambda c: (0, jnp.where(c[0] > 0, fused(*args), c[1])), (bad, kept)
    )[1]
    return result.reshape(result.shape[0], 1, result.shape[1])


def lookup(lookup_table, at_index):
    count = lookup_table.shape[0]
    hits = jnp.arange(count, dtype=jnp.int32) == at_index[..., None]
    return jnp.sum(jnp.where(hits, lookup_table, 0), axis=-1)


def per_device(queries, image_keys, image_values, head_gate, token_image, span_first, image_slot):
    tensor_count = lax.axis_size("tensor")
    row_count = queries.shape[0]
    half_width = queries.shape[2]
    split_rows = queries.reshape(row_count, tensor_count, half_width // tensor_count)
    head_rows = lax.all_to_all(split_rows, "tensor", split_axis=1, concat_axis=0, tiled=True)
    token_count = head_rows.shape[0]
    head_width = head_rows.shape[2]
    head_count = head_width // DH
    held_count = image_keys.shape[0]
    latents = image_keys.shape[1]
    images = image_slot.shape[0]
    packed = jnp.concatenate([image_keys[:, :, 0, :], image_values[:, :, 0, :]], axis=2)
    packed = packed.reshape(held_count, latents * 2 * head_width)
    window_start = jnp.minimum(token_image[0], images - MAXIMG)
    window_ids = window_start + jnp.arange(MAXIMG, dtype=jnp.int32)
    in_window = window_ids < images
    safe_ids = jnp.minimum(window_ids, images - 1)
    window_slot = lookup(image_slot, safe_ids)
    fragment = lax.all_gather(packed, "seq", axis=0, tiled=True)
    piece_rows = jnp.arange(fragment.shape[0], dtype=jnp.int32)
    select = ((window_slot[:, None] == piece_rows[None, :]) & in_window[:, None]).astype(
        jnp.bfloat16
    )
    window = jnp.dot(select, fragment, preferred_element_type=jnp.float32).astype(jnp.bfloat16)
    window = window.reshape(MAXIMG * latents, 2 * head_width)
    keys_win = window[:, :head_width]
    values_win = window[:, head_width:]
    visible = (window_ids[None, :] >= span_first[:, None]) & (
        window_ids[None, :] <= token_image[:, None]
    )
    key_mask = jnp.repeat(visible, latents, axis=1)
    score_scale = 1.0 / math.sqrt(DH)
    gate_values = jnp.tanh(head_gate.reshape(-1))
    results = []
    for head_index in range(head_count):
        low_col = head_index * DH
        head_query = head_rows[:, 0, low_col : low_col + DH]
        scores = (
            lax.dot_general(
                head_query,
                keys_win[:, low_col : low_col + DH],
                (((1,), (1,)), ((), ())),
                preferred_element_type=jnp.float32,
            )
            * score_scale
        )
        row_top = jnp.max(jnp.where(key_mask, scores, -1e30), axis=1, keepdims=True)
        raised = jnp.exp(jnp.where(key_mask, scores - row_top, -1e30))
        row_total = jnp.sum(raised, axis=1, keepdims=True)
        weights = raised.astype(jnp.bfloat16)
        summed = jnp.dot(
            weights, values_win[:, low_col : low_col + DH], preferred_element_type=jnp.float32
        )
        results.append(summed / row_total * gate_values[head_index])
    attended = jnp.concatenate(results, axis=1).astype(jnp.bfloat16)
    return attended.reshape(token_count, 1, head_width)


def solution(mesh):
    placed = (
        P(("groups", "seq", "tensor"), "sub", None),
        P(("groups", "seq"), None, "sub", "tensor"),
        P(("groups", "seq"), None, "sub", "tensor"),
        P("sub", "tensor"),
        P(("groups", "seq")),
        P(("groups", "seq")),
        P("groups"),
    )
    fits = mesh.shape["seq"] == 4 and mesh.shape["tensor"] == 2
    return jax.shard_map(
        attended if fits else per_device,
        mesh=mesh,
        in_specs=placed,
        out_specs=P(("groups", "seq"), "sub", "tensor"),
        check_vma=False,
    )
```
